512 devices in a mesh: gx: 4 (over z_lo), gy: 4 (over z_hi, core), vert: 32 (over y, x).
Axes of the slice: x: 4, y: 8, z: 8 (z_hi: 2, z_lo: 4; z = z_hi * 4 + z_lo), core: 2. Of those that a mesh axis runs over, the one named last changes fastest.
Arguments:
- distribution: float32 [1024, 16, 32, 128], P('vert', 'gx', 'gy'), may hold values from -6 to 6
- vel_index: int32 [3, 1024], P(None, 'vert'), may hold values from 0 to 7
- signs: int32 [3, 1024], P(None, 'vert'), may hold values from 0 to 1
- cell_type: int32 [16, 32, 128], P('gx', 'gy'), may hold values 0 or 1
- coupling: float32 [5, 8], replicated, may hold values from -2 to 2
Outputs:
- relaxed: float32 [1024, 16, 32, 128], P('vert', 'gx', 'gy')
The draws below stay inside these ranges and needn't reach their ends.
All inputs are finite; a program needn't handle non-finite values. No bound on the sum of `cell_type` on one device may be relied on, other than what follows from the above.
Results may differ from the reference program's by a relative error of at most 0.0001.
Values sent between devices are 32-bit elements; how exact they have to be, the bound alone decides.
No kernel may reach another device: no remote copies, remote signals or barrier semaphores. Data moves between devices by JAX's collectives and lax.ppermute only.
A program may use at most 64 MiB of HBM per device.

```python
import jax
import jax.numpy as jnp
from jax import lax

V = 1024
SPEEDS = 8
NZ = 128
ITERS = 2
NX = 16
NY = 32


def plant(result, key, smallest, largest):
    longest = result.shape.index(max(result.shape))
    spots = []
    for shift in (0, 1):
        where = [jax.random.randint(jax.random.fold_in(key, axis), (), 0, length) for axis, length in enumerate(result.shape)]
        where[longest] = (where[longest] + shift) % result.shape[longest]
        spots.append(tuple(where))
    return result.at[spots[0]].set(smallest).at[spots[1]].set(largest)


def levels(own_key, shape, split, low, high):
    loudness = 1.0
    for dim, parts in split:
        heights = jax.random.uniform(jax.random.fold_in(jax.random.fold_in(own_key, 6), dim), (parts,), jnp.float32, low / len(split), high / len(split))
        loudness = loudness * jnp.repeat(jnp.exp(heights), shape[dim] // parts).reshape((-1,) + (1,) * (len(shape) - 1 - dim))
    return loudness


def centred(key, extent, deviation, reach, cuts=(), dtype=jnp.bfloat16):
    array = deviation * jax.random.normal(key, extent, jnp.float32)
    if cuts:
        array = array * levels(key, extent, cuts, -0.22, 0.18)
    return jnp.clip(array, -reach, reach).astype(dtype)


def setup_inputs(seed: int = 0) -> dict:
    keys = jax.random.split(jax.random.key(seed), 6)
    distribution = centred(keys[0], (V, NX, NY, NZ), 1.0, 6.0, ((0, 32), (1, 4), (2, 4)), jnp.float32)
    vel_index = plant(jax.random.randint(keys[1], (3, V), 0, SPEEDS), jax.random.fold_in(keys[1], 1), 0, SPEEDS - 1).astype(jnp.int32)
    signs = plant(jax.random.randint(keys[2], (3, V), 0, 2), jax.random.fold_in(keys[2], 1), 0, 1).astype(jnp.int32)
    cell_type = plant((jax.random.randint(keys[3], (NX, NY, NZ), 0, 8) < 1).astype(jnp.int32), jax.random.fold_in(keys[3], 1), 0, 1)
    coupling = centred(keys[4], (5, 8), 8 ** -0.5, 2.0, (), jnp.float32)
    return dict(distribution=distribution, vel_index=vel_index, signs=signs, cell_type=cell_type, coupling=coupling)


absorb = 0.5
diffuse = 1.0
damping = 0.8
cfl_ratio = 0.2
relax_rate = 0.5
prandtl = 2.0 / 3.0


def velocity_tables(vel_index, signs, total):
    speeds = (vel_index.astype(jnp.float32) + 0.5) * 0.25
    direction = signs.astype(jnp.float32) * 2.0 - 1.0
    veloc = speeds * direction
    square = jnp.sum(veloc * veloc, axis=0)
    weight = 64.0 * jnp.exp(-square) / total
    vel_x, vel_y, vel_z = veloc[0], veloc[1], veloc[2]
    unit_row = jnp.ones_like(vel_x)
    heat_term = square - 2.5
    moment_basis = jnp.stack([unit_row, vel_x, vel_y, vel_z, square - 1.5, vel_x * vel_y, vel_x * vel_z,
                              vel_y * vel_z, vel_x * vel_x - vel_y * vel_y, vel_y * vel_y - vel_z * vel_z,
                              heat_term * vel_x, heat_term * vel_y, heat_term * vel_z]) * weight[None]
    shakhov = 0.8 * (1.0 - prandtl)
    equil_table = jnp.stack([unit_row, 2.0 * vel_x, 2.0 * vel_y, 2.0 * vel_z, (2.0 / 3.0) * (square - 1.5),
                             shakhov * heat_term * vel_x, shakhov * heat_term * vel_y,
                             shakhov * heat_term * vel_z], axis=1)
    return veloc, direction, moment_basis, equil_table


def neighbours(field):
    total = jnp.roll(field, 1, axis=1) + jnp.roll(field, -1, axis=1)
    total = total + jnp.roll(field, 1, axis=2) + jnp.roll(field, -1, axis=2)
    return total + jnp.roll(field, 1, axis=3) + jnp.roll(field, -1, axis=3)


def two_grid(source):
    fine_diag = absorb + 6.0 * diffuse
    coarse_diag = absorb + 1.5 * diffuse
    first = damping * source / fine_diag
    resid = source - (fine_diag * first - diffuse * neighbours(first))
    field_count, size_x, size_y, size_z = resid.shape
    blocked = (field_count, size_x // 2, 2, size_y // 2, 2, size_z // 2, 2)
    coarse_res = resid.reshape(blocked).mean(axis=(2, 4, 6))
    coarse_one = damping * coarse_res / coarse_diag
    applied = coarse_diag * coarse_one - 0.25 * diffuse * neighbours(coarse_one)
    coarse_two = coarse_one + damping * (coarse_res - applied) / coarse_diag
    widened = jnp.broadcast_to(coarse_two[:, :, None, :, None, :, None], blocked).reshape(resid.shape)
    second = first + widened
    return second + damping * (source - (fine_diag * second - diffuse * neighbours(second))) / fine_diag


def upwind(centre, axis, upper):
    back_one = jnp.roll(centre, 1, axis=axis)
    back_two = jnp.roll(centre, 2, axis=axis)
    front_one = jnp.roll(centre, -1, axis=axis)
    front_two = jnp.roll(centre, -2, axis=axis)
    backward = 1.5 * centre - 2.0 * back_one + 0.5 * back_two
    forward = -1.5 * centre + 2.0 * front_one - 0.5 * front_two
    return upper * backward + (1.0 - upper) * forward


def reference(distribution, vel_index, signs, cell_type, coupling):
    veloc, direction, moment_basis, equil_table = velocity_tables(vel_index, signs, V)
    block = 32
    count = V // block
    cells = NX * NY * NZ
    wall = cell_type[None] == 1
    basis_blocks = moment_basis.reshape(13, count, block).transpose(1, 0, 2)
    equil_blocks = equil_table.reshape(count, block, 8)
    vel_blocks = veloc.reshape(3, count, block).transpose(1, 0, 2)
    upper_blocks = ((direction + 1.0) * 0.5).reshape(3, count, block).transpose(1, 0, 2)
    for sweep_index in range(ITERS):
        shaped = distribution.reshape(count, block, cells)

        def accumulate(total, operands):
            return total + jnp.dot(operands[0], operands[1], precision=lax.Precision.HIGHEST), None

        moments, unused = lax.scan(accumulate, jnp.zeros((13, cells), jnp.float32), (basis_blocks, shaped))
        conserved = absorb * moments[0:5] + jnp.dot(coupling, moments[5:13], precision=lax.Precision.HIGHEST)
        corrected = two_grid(conserved.reshape(5, NX, NY, NZ))
        fields = jnp.concatenate([corrected.reshape(5, cells), moments[10:13]], axis=0)

        def advance(operands):
            dist_block, equil_block, vel_block, upper_block = operands
            feq = jnp.dot(equil_block, fields, precision=lax.Precision.HIGHEST).reshape(block, NX, NY, NZ)
            advect = jnp.zeros_like(dist_block)
            for axis_number in range(3):
                vel_col = vel_block[axis_number][:, None, None, None]
                upper = upper_block[axis_number][:, None, None, None]
                advect = advect + vel_col * upwind(dist_block, axis_number + 1, upper)
            half = dist_block + relax_rate * (feq - dist_block) - cfl_ratio * advect
            return jnp.where(wall, feq, half)

        updated = lax.map(advance, (distribution.reshape(count, block, NX, NY, NZ), equil_blocks,
                                    vel_blocks, upper_blocks))
        distribution = updated.reshape(V, NX, NY, NZ)
    return distribution
```

```python
import jax
import jax.numpy as jnp
import numpy as np
from jax import lax
from jax.experimental import pallas as pl
from jax.experimental.pallas import tpu as pltpu
from jax.sharding import PartitionSpec as P

V = 1024
INTERPRET = False

absorb = 0.5
damping = 0.8
fine_diag = 6.5
prandtl = 2.0 / 3.0

SX, SY, NZ = 4, 8, 128
COLS = SX * SY
ROWS = 8
LANES = ROWS * COLS
BLOCKS = 16
WIN = 24
WIN2 = 16
F32 = jnp.float32


def roll(x, shift, axis):
    return pltpu.roll(x, shift % x.shape[axis], axis)


def iota(shape, dim):
    return lax.broadcasted_iota(jnp.int32, shape, dim)


def velocity_tables(vel_index, signs, coupling):
    speeds = (vel_index.astype(F32) + 0.5) * 0.25
    positive = signs.astype(F32)
    veloc = speeds * (positive * 2.0 - 1.0)
    square = jnp.sum(veloc * veloc, axis=0)
    weight = 64.0 * jnp.exp(-square) / V
    vel_x, vel_y, vel_z = (veloc[0], veloc[1], veloc[2])
    unit_row = jnp.ones_like(vel_x)
    heat_term = square - 2.5
    basis = (
        jnp.stack(
            [
                unit_row,
                vel_x,
                vel_y,
                vel_z,
                square - 1.5,
                vel_x * vel_y,
                vel_x * vel_z,
                vel_y * vel_z,
                vel_x * vel_x - vel_y * vel_y,
                vel_y * vel_y - vel_z * vel_z,
                heat_term * vel_x,
                heat_term * vel_y,
                heat_term * vel_z,
            ]
        )
        * weight[None]
    )
    shakhov = 0.8 * (1.0 - prandtl)
    equil = jnp.stack(
        [
            unit_row,
            2.0 * vel_x,
            2.0 * vel_y,
            2.0 * vel_z,
            2.0 / 3.0 * (square - 1.5),
            shakhov * heat_term * vel_x,
            shakhov * heat_term * vel_y,
            shakhov * heat_term * vel_z,
        ]
    )
    mixed = jnp.sum(coupling[:, :, None] * basis[None, 5:13], axis=1)
    source_basis = jnp.concatenate([absorb * basis[0:5] + mixed, basis[10:13]], axis=0)
    centre = 0.5 - 0.3 * jnp.sum(speeds, axis=0)
    table = jnp.concatenate(
        [
            source_basis,
            equil,
            centre[None],
            0.4 * speeds * positive,
            0.4 * speeds * (1.0 - positive),
            jnp.zeros_like(centre)[None],
        ],
        axis=0,
    ).T
    cross = jnp.sum(source_basis[:, None] * equil[None], axis=2)
    cross_row = jnp.pad(cross, ((0, 0), (0, COLS - ROWS))).reshape(1, LANES)
    return table, cross_row


def moments(src, table, m_scr, ext):
    zero = jnp.zeros((SY, NZ), F32)

    def step(v, accs):
        tiles = [src[v, x] for x in range(SX)]
        out = []
        for r in range(ROWS):
            w = table[v, r]
            out += [accs[r * SX + x] + w * tiles[x] for x in range(SX)]
        return tuple(out)

    accs = lax.fori_loop(0, src.shape[0], step, (zero,) * (ROWS * SX), unroll=2)
    for i, acc in enumerate(accs):
        m_scr[i * SY : (i + 1) * SY, :] = acc
    for h in range(2):
        turned = m_scr[h * 128 : (h + 1) * 128, :].T
        lanes = slice(h * 128, (h + 1) * 128)
        ext[16:144, lanes] = turned
        ext[0:16, lanes] = turned[112:128]
        ext[144:168, lanes] = turned[0:24]


def first_kernel(table, f, win, north, south, m_scr, ext):
    moments(f, table, m_scr, ext)
    for j in range(win.shape[0]):
        win[j] = ext[4 * j + 6 : 4 * j + 6 + WIN, :]
    pack_rows(f, north, south)


def pack_rows(src, north, south):
    pair = iota((SY, NZ), 0) // 2

    def step(v, carry):
        top = roll(src[v, 0], 0, 0)
        low = roll(src[v, 0], -6, 0)
        for x in range(1, SX):
            tile = src[v, x]
            top = jnp.where(pair == x, roll(tile, 2 * x, 0), top)
            low = jnp.where(pair == x, roll(tile, 2 * x - 6, 0), low)
        north[v] = top
        south[v] = low
        return carry

    lax.fori_loop(0, src.shape[0], step, 0, unroll=4)


def row_halo(north, south, x, sub):
    return jnp.where(sub < 4, roll(north, -2 * x, 0), roll(south, 6 - 2 * x, 0))


def transport(table, v, tiles, edges, sub):
    centre = table[v, 16]
    up = [table[v, 17 + d] for d in range(3)]
    down = [table[v, 20 + d] for d in range(3)]
    out = []
    for x in range(SX):
        f = tiles[x + 2]
        e = edges[x]
        acc = centre * f
        acc += up[0] * (tiles[x + 1] - 0.25 * tiles[x])
        acc += down[0] * (tiles[x + 3] - 0.25 * tiles[x + 4])
        back_one = roll(jnp.where(sub >= 7, e, f), 1, 0)
        back_two = roll(jnp.where(sub >= 6, e, f), 2, 0)
        front_one = roll(jnp.where(sub < 1, e, f), -1, 0)
        front_two = roll(jnp.where(sub < 2, e, f), -2, 0)
        acc += up[1] * (back_one - 0.25 * back_two)
        acc += down[1] * (front_one - 0.25 * front_two)
        acc += up[2] * (roll(f, 1, 1) - 0.25 * roll(f, 2, 1))
        acc += down[2] * (roll(f, -1, 1) - 0.25 * roll(f, -2, 1))
        out.append(acc)
    return out


def second_kernel(table, f, low, high, north, south, fluid, cross, g, win, g_north, g_south, m_scr, ext):
    sub = iota((SY, NZ), 0)

    def step(v, carry):
        tiles = [low[v, 0], low[v, 1]] + [f[v, x] for x in range(SX)] + [high[v, 0], high[v, 1]]
        above, below = north[v], south[v]
        edges = [row_halo(above, below, x, sub) for x in range(SX)]
        moved = transport(table, v, tiles, edges, sub)
        for x in range(SX):
            g[v, x] = fluid[x] * moved[x]
        return carry

    lax.fori_loop(0, f.shape[0], step, 0, unroll=2)
    moments(g, table, m_scr, ext)
    for j in range(win.shape[0]):
        win[j] = ext[4 * j + 10 : 4 * j + 10 + WIN2, :]
        win[j, 0:1, :] = cross[...]
    pack_rows(g, g_north, g_south)


def solve_kernel(place, recv, coef, out, src, coarse, fine, gain, extra, first, msg):
    shape = (2 * WIN, 128)
    lane = iota(shape, 1)
    x_at = (lane // SY) % SX
    y_at = lane % SY
    z_odd = iota(shape, 0) % 2
    is_field = (iota(shape, 0) // WIN) * 4 + lane // COLS < 5
    tile_sub = iota((8, 128), 0)
    tile_lane = iota((8, 128), 1)

    def unpack(i, carry):
        for h in range(2):
            lanes = slice(h * 128, (h + 1) * 128)
            src[i, h * WIN : (h + 1) * WIN, :] = recv[i, 0:WIN, lanes]
            extra[i, h * WIN : h * WIN + 4, :] = jnp.zeros((4, 128), F32)
            extra[i, h * WIN + 20 : (h + 1) * WIN, :] = jnp.zeros((4, 128), F32)
            extra[i, h * WIN + 4 : h * WIN + 20, :] = recv[i, WIN : WIN + WIN2, lanes]
        gain[i] = jnp.zeros(shape, F32)
        for half, at in enumerate((WIN, WIN + WIN2 - 1)):
            left = jnp.broadcast_to(recv[i, at : at + 1, 0:128], (8, 128))
            right = jnp.broadcast_to(recv[i, at : at + 1, 128:256], (8, 128))
            t = jnp.where(tile_sub < 4, left, right)
            t = jnp.where(tile_lane // COLS == tile_sub % 4, t, 0.0)
            t = t + roll(t, 32, 1)
            t = t + roll(t, 64, 1)
            for h in range(2):
                gain[i, h * WIN + 4 + 8 * half : h * WIN + 12 + 8 * half, :] = t
        return carry

    lax.fori_loop(0, BLOCKS, unpack, 0)

    def around(i):
        gx, gy = i // 4, i % 4
        return (
            ((gx + 1) % 4) * 4 + gy,
            ((gx + 3) % 4) * 4 + gy,
            gx * 4 + (gy + 1) % 4,
            gx * 4 + (gy + 3) % 4,
        )

    def neighbours(ref, i, step):
        next_x, last_x, next_y, last_y = around(i)
        c = ref[i]
        dx, dy = SY * step, step
        total = jnp.where(x_at < SX - step, roll(c, -dx, 1), roll(ref[next_x], COLS - dx, 1))
        total += jnp.where(x_at >= step, roll(c, dx, 1), roll(ref[last_x], dx - COLS, 1))
        total += jnp.where(y_at < SY - step, roll(c, -dy, 1), roll(ref[next_y], SY - dy, 1))
        total += jnp.where(y_at >= step, roll(c, dy, 1), roll(ref[last_y], dy - SY, 1))
        return total + roll(c, step, 0) + roll(c, -step, 0)

    def restrict(i, carry):
        r = (1.0 - damping) * src[i] + (damping / fine_diag) * neighbours(src, i, 1)
        r = r + jnp.where(x_at % 2 == 0, roll(r, -SY, 1), roll(r, SY, 1))
        r = r + jnp.where(y_at % 2 == 0, roll(r, -1, 1), roll(r, 1, 1))
        r = r + jnp.where(z_odd == 0, roll(r, -1, 0), roll(r, 1, 0))
        coarse[i] = 0.125 * r
        return carry

    def correct(i, carry):
        two = 0.48 * coarse[i] + 0.04 * neighbours(coarse, i, 2)
        fine[i] = (damping / fine_diag) * src[i] + two
        return carry

    def smooth(i):
        y = (1.0 - damping) * fine[i] + (damping / fine_diag) * (src[i] + neighbours(fine, i, 1))
        return jnp.where(is_field, y, src[i])

    def mix(i, carry):
        field = smooth(i)
        first[i] = gain[i] * field
        parts = (field[0:WIN], field[WIN : 2 * WIN])
        here = lane[0:WIN]
        sums = [0.0, 0.0]
        for b in range(4):
            turned = [roll(p, -COLS * b, 1) for p in parts]
            near = here < 128 - COLS * b
            same = [
                jnp.where(near, turned[0], turned[1]),
                jnp.where(near, turned[1], turned[0]),
            ]
            for h in range(2):
                lanes = slice(h * 128, (h + 1) * 128)
                sums[h] = (
                    sums[h]
                    + coef[b : b + 1, lanes] * same[h]
                    + coef[4 + b : 5 + b, lanes] * same[1 - h]
                )
        for h in range(2):
            rows = slice(h * WIN, (h + 1) * WIN)
            coarse[i, rows, :] = gain[i, rows, :] * sums[h] + extra[i, rows, :]
        return carry

    def swap(i, carry):
        src[i] = coarse[i]
        return carry

    lax.fori_loop(0, BLOCKS, restrict, 0)
    lax.fori_loop(0, BLOCKS, correct, 0)
    lax.fori_loop(0, BLOCKS, mix, 0)
    lax.fori_loop(0, BLOCKS, swap, 0)
    lax.fori_loop(0, BLOCKS, restrict, 0)
    own = place[0]
    next_x, last_x, next_y, last_y = around(own)
    for i in (own, next_x, last_x, next_y, last_y):
        correct(i, 0)
    second = gain[own] * smooth(own)
    side_x = jnp.where(x_at < 2, roll(first[last_x], -16, 1), roll(first[next_x], 16, 1))
    side_y = jnp.where(y_at < 4, first[next_y], first[last_y])
    pieces = ((first[own], side_x), (side_y, second))
    for k in range(2):
        for m in range(2):
            for h in range(2):
                at = (2 * m + h) * 128
                coarse[0] = pieces[k][m]
                msg[4 * k : 4 * k + 4, at : at + 128] = coarse[0, h * WIN + 10 : h * WIN + 14, :]
    for j in range(out.shape[0]):
        out[j] = msg[...]


def last_kernel(table, recv, g, low, high, north, south, fluid, out, turn, fields):
    for j in range(recv.shape[0]):
        turn[4 * j : 4 * j + 4, 0:512] = recv[j, 0:4, :]
        turn[4 * j : 4 * j + 4, 512:1024] = recv[j, 4:8, :]
    for k in range(8):
        block = turn[:, k * 128 : (k + 1) * 128].T
        for r in range(4):
            for x in range(SX):
                at = (r * SX + x) * SY
                fields[k // 2, (k % 2) * 4 + r, x] = block[at : at + SY]
    sub = iota((SY, NZ), 0)

    def step(v, carry):
        psi = [table[v, ROWS + r] for r in range(ROWS)]

        def lift(part, x):
            total = psi[0] * fields[part, 0, x]
            for r in range(1, ROWS):
                total += psi[r] * fields[part, r, x]
            return total

        above, below = north[v], south[v]
        tiles = [lift(1, x) + low[v, x] for x in range(2)]
        tiles += [lift(0, x) + g[v, x] for x in range(SX)]
        tiles += [lift(1, 2 + x) + high[v, x] for x in range(2)]
        edges = [lift(2, x) + row_halo(above, below, x, sub) for x in range(SX)]
        moved = transport(table, v, tiles, edges, sub)
        for x in range(SX):
            out[v, x] = fluid[x] * moved[x] + lift(3, x)
        return carry

    lax.fori_loop(0, out.shape[0], step, 0)


VMEM = pltpu.MemorySpace.VMEM
SMEM = pltpu.MemorySpace.SMEM


def call(kernel, spaces, outs, scratch):
    specs = [pl.BlockSpec(memory_space=s) for s in spaces]
    shapes = [jax.ShapeDtypeStruct(s, F32) for s in outs]
    return pl.pallas_call(
        kernel,
        in_specs=specs,
        out_specs=[pl.BlockSpec(memory_space=VMEM) for _ in outs],
        out_shape=shapes,
        scratch_shapes=[pltpu.VMEM(s, F32) for s in scratch],
        interpret=INTERPRET,
        name=kernel.__name__,
    )


def stage_first(f, table, members):
    vels = f.shape[0]
    return call(
        first_kernel,
        (SMEM, VMEM),
        ((members, WIN, LANES), (vels, SY, NZ), (vels, SY, NZ)),
        ((LANES, NZ), (168, LANES)),
    )(table, f)


def stage_second(f, table, low, high, north, south, fluid, cross, members):
    vels = f.shape[0]
    return call(
        second_kernel,
        (SMEM,) + (VMEM,) * 7,
        (f.shape, (members, WIN2, LANES), (vels, SY, NZ), (vels, SY, NZ)),
        ((LANES, NZ), (168, LANES)),
    )(table, f, low, high, north, south, fluid, cross)


def wall_rows(cell_type, member):
    gain = jnp.where(cell_type == 1, 1.0, 0.5).astype(F32).reshape(COLS, NZ).T
    wrapped = jnp.concatenate([gain[NZ - 8 :], gain, gain[:16]], axis=0)
    return lax.dynamic_slice_in_dim(wrapped, 4 * member + 2, WIN2, axis=0).reshape(2, LANES)


def stage_middle(got_one, got_two, walls):
    one = jnp.sum(got_one, axis=0)
    two = jnp.sum(got_two, axis=0)
    whole = jnp.concatenate([one, walls[0:1], two[1 : WIN2 - 1], walls[1:2]], axis=0)
    cross = two[0].reshape(ROWS, COLS)[:, :ROWS]
    pick = np.zeros((ROWS, ROWS, ROWS), np.float32)
    for k in range(ROWS):
        for r in range(ROWS):
            pick[k, r, (r + k) % ROWS] = 1.0
    coef = jnp.sum(jnp.asarray(pick) * cross[None], axis=2)
    coef = jnp.broadcast_to(coef[:, :, None], (ROWS, ROWS, COLS)).reshape(ROWS, LANES)
    return jnp.broadcast_to(whole[None], (BLOCKS,) + whole.shape), coef


def stage_solve(place, got, coef, members):
    big = (BLOCKS, 2 * WIN, 128)
    return call(
        solve_kernel,
        (SMEM, VMEM, VMEM),
        ((members, 8, 512),),
        (big,) * 6 + ((8, 512),),
    )(place, got, coef)[0]


def stage_last(table, got, g, low, high, north, south, fluid):
    return call(
        last_kernel,
        (SMEM,) + (VMEM,) * 7,
        (g.shape,),
        ((NZ, 1024), (4, ROWS, SX, SY, NZ)),
    )(table, got, g, low, high, north, south, fluid)[0]


def halos(f, north, south):
    def ring(axis, step):
        count = lax.axis_size(axis)
        return [(i, (i + step) % count) for i in range(count)]

    low = lax.ppermute(f[:, SX - 2 :], "gx", ring("gx", 1))
    high = lax.ppermute(f[:, :2], "gx", ring("gx", -1))
    above = lax.ppermute(north, "gy", ring("gy", -1))
    below = lax.ppermute(south, "gy", ring("gy", 1))
    return low, high, above, below


def swap_all(x, axis):
    return lax.all_to_all(x, axis, 0, 0, tiled=True)


def local(f, vel_index, signs, cell_type, coupling):
    members = lax.axis_size("vert")
    table, cross = velocity_tables(vel_index, signs, coupling)
    fluid = jnp.where(cell_type == 1, 0.0, 1.0).astype(F32)
    walls = wall_rows(cell_type, lax.axis_index("vert"))
    place = (lax.axis_index("gx") * 4 + lax.axis_index("gy")).astype(jnp.int32).reshape(1)
    win_one, north, south = stage_first(f, table, members)
    got_one = swap_all(win_one, "vert")
    near = halos(f, north, south)
    g, win_two, north, south = stage_second(f, table, *near, fluid, cross, members)
    got_two = swap_all(win_two, "vert")
    near = halos(g, north, south)
    whole, coef = stage_middle(got_one, got_two, walls)
    got = swap_all(whole, ("gx", "gy"))
    sent = stage_solve(place, got, coef, members)
    got = swap_all(sent, "vert")
    return stage_last(table, got, g, *near, fluid)


def solution(mesh):
    in_specs = (
        P("vert", "gx", "gy", None),
        P(None, "vert"),
        P(None, "vert"),
        P("gx", "gy", None),
        P(),
    )
    out_specs = P("vert", "gx", "gy", None)
    return jax.shard_map(local, mesh=mesh, in_specs=in_specs, out_specs=out_specs, check_vma=False)
```

```python
import jax
import jax.numpy as jnp
import numpy as np
from jax import lax
from jax.experimental import pallas as pl
from jax.experimental.pallas import tpu as pltpu
from jax.sharding import PartitionSpec as P

V = 1024
INTERPRET = False
UNROLL = 4

absorb = 0.5
damping = 0.8
fine_diag = 6.5
prandtl = 2.0 / 3.0

SX, SY, NZ = 4, 8, 128
COLS = SX * SY
ROWS = 8
LANES = ROWS * COLS
BLOCKS = 16
WIN = 24
WIN2 = 16
F32 = jnp.float32


def roll(x, shift, axis):
    return pltpu.roll(x, shift % x.shape[axis], axis)


def iota(shape, dim):
    return lax.broadcasted_iota(jnp.int32, shape, dim)


def velocity_tables(vel_index, signs, coupling):
    speeds = (vel_index.astype(F32) + 0.5) * 0.25
    positive = signs.astype(F32)
    veloc = speeds * (positive * 2.0 - 1.0)
    square = jnp.sum(veloc * veloc, axis=0)
    weight = 64.0 * jnp.exp(-square) / V
    vel_x, vel_y, vel_z = (veloc[0], veloc[1], veloc[2])
    unit_row = jnp.ones_like(vel_x)
    heat_term = square - 2.5
    basis = (
        jnp.stack(
            [
                unit_row,
                vel_x,
                vel_y,
                vel_z,
                square - 1.5,
                vel_x * vel_y,
                vel_x * vel_z,
                vel_y * vel_z,
                vel_x * vel_x - vel_y * vel_y,
                vel_y * vel_y - vel_z * vel_z,
                heat_term * vel_x,
                heat_term * vel_y,
                heat_term * vel_z,
            ]
        )
        * weight[None]
    )
    shakhov = 0.8 * (1.0 - prandtl)
    equil = jnp.stack(
        [
            unit_row,
            2.0 * vel_x,
            2.0 * vel_y,
            2.0 * vel_z,
            2.0 / 3.0 * (square - 1.5),
            shakhov * heat_term * vel_x,
            shakhov * heat_term * vel_y,
            shakhov * heat_term * vel_z,
        ]
    )
    mixed = jnp.sum(coupling[:, :, None] * basis[None, 5:13], axis=1)
    source_basis = jnp.concatenate([absorb * basis[0:5] + mixed, basis[10:13]], axis=0)
    centre = 0.5 - 0.3 * jnp.sum(speeds, axis=0)
    table = jnp.concatenate(
        [
            source_basis,
            equil,
            centre[None],
            0.4 * speeds * positive,
            0.4 * speeds * (1.0 - positive),
            jnp.zeros_like(centre)[None],
        ],
        axis=0,
    )
    cross = jnp.sum(source_basis[:, None] * equil[None], axis=2)
    cross_row = jnp.pad(cross, ((0, 0), (0, COLS - ROWS))).reshape(1, LANES)
    return table, cross_row


def moments(src, table, m_scr, ext):
    zero = jnp.zeros((SY, NZ), F32)

    def step(v, accs):
        tiles = [src[v, x] for x in range(SX)]
        out = []
        for r in range(ROWS):
            w = table[r, v]
            out += [accs[r * SX + x] + w * tiles[x] for x in range(SX)]
        return tuple(out)

    accs = lax.fori_loop(0, src.shape[0], step, (zero,) * (ROWS * SX), unroll=2)
    for i, acc in enumerate(accs):
        m_scr[i * SY : (i + 1) * SY, :] = acc
    for h in range(2):
        turned = m_scr[h * 128 : (h + 1) * 128, :].T
        lanes = slice(h * 128, (h + 1) * 128)
        ext[16:144, lanes] = turned
        ext[0:16, lanes] = turned[112:128]
        ext[144:168, lanes] = turned[0:24]


def first_kernel(table, f, win, north, south, m_scr, ext):
    moments(f, table, m_scr, ext)
    for j in range(win.shape[0]):
        win[j] = ext[4 * j + 6 : 4 * j + 6 + WIN, :]
    pack_rows(f, north, south)


def pack_rows(src, north, south):
    pair = iota((SY, NZ), 0) // 2

    def step(v, carry):
        top = roll(src[v, 0], 0, 0)
        low = roll(src[v, 0], -6, 0)
        for x in range(1, SX):
            tile = src[v, x]
            top = jnp.where(pair == x, roll(tile, 2 * x, 0), top)
            low = jnp.where(pair == x, roll(tile, 2 * x - 6, 0), low)
        north[v] = top
        south[v] = low
        return carry

    lax.fori_loop(0, src.shape[0], step, 0, unroll=4)


def row_halo(north, south, x, sub):
    return jnp.where(sub < 4, roll(north, -2 * x, 0), roll(south, 6 - 2 * x, 0))


def transport(table, v, tiles, edges, sub):
    centre = table[16, v]
    up = [table[17 + d, v] for d in range(3)]
    down = [table[20 + d, v] for d in range(3)]
    out = []
    for x in range(SX):
        f = tiles[x + 2]
        e = edges[x]
        acc = centre * f
        acc += up[0] * (tiles[x + 1] - 0.25 * tiles[x])
        acc += down[0] * (tiles[x + 3] - 0.25 * tiles[x + 4])
        back_one = roll(jnp.where(sub >= 7, e, f), 1, 0)
        back_two = roll(jnp.where(sub >= 6, e, f), 2, 0)
        front_one = roll(jnp.where(sub < 1, e, f), -1, 0)
        front_two = roll(jnp.where(sub < 2, e, f), -2, 0)
        acc += up[1] * (back_one - 0.25 * back_two)
        acc += down[1] * (front_one - 0.25 * front_two)
        acc += up[2] * (roll(f, 1, 1) - 0.25 * roll(f, 2, 1))
        acc += down[2] * (roll(f, -1, 1) - 0.25 * roll(f, -2, 1))
        out.append(acc)
    return out


def second_kernel(table, f, low, high, north, south, fluid, cross, g, win, g_north, g_south, m_scr, ext):
    sub = iota((SY, NZ), 0)

    def step(v, carry):
        tiles = [low[v, 0], low[v, 1]] + [f[v, x] for x in range(SX)] + [high[v, 0], high[v, 1]]
        above, below = north[v], south[v]
        edges = [row_halo(above, below, x, sub) for x in range(SX)]
        moved = transport(table, v, tiles, edges, sub)
        for x in range(SX):
            g[v, x] = fluid[x] * moved[x]
        return carry

    lax.fori_loop(0, f.shape[0], step, 0, unroll=2)
    moments(g, table, m_scr, ext)
    for j in range(win.shape[0]):
        win[j] = ext[4 * j + 10 : 4 * j + 10 + WIN2, :]
        win[j, 0:1, :] = cross[...]
    pack_rows(g, g_north, g_south)


def solve_kernel(place, recv, coef, out, src, coarse, fine, gain, extra, first, msg):
    shape = (2 * WIN, 128)
    lane = iota(shape, 1)
    x_at = (lane // SY) % SX
    y_at = lane % SY
    z_odd = iota(shape, 0) % 2
    is_field = (iota(shape, 0) // WIN) * 4 + lane // COLS < 5
    tile_sub = iota((8, 128), 0)
    tile_lane = iota((8, 128), 1)

    def unpack(i, carry):
        for h in range(2):
            lanes = slice(h * 128, (h + 1) * 128)
            src[i, h * WIN : (h + 1) * WIN, :] = recv[i, 0:WIN, lanes]
            extra[i, h * WIN : h * WIN + 4, :] = jnp.zeros((4, 128), F32)
            extra[i, h * WIN + 20 : (h + 1) * WIN, :] = jnp.zeros((4, 128), F32)
            extra[i, h * WIN + 4 : h * WIN + 20, :] = recv[i, WIN : WIN + WIN2, lanes]
        gain[i] = jnp.zeros(shape, F32)
        for half, at in enumerate((WIN, WIN + WIN2 - 1)):
            left = jnp.broadcast_to(recv[i, at : at + 1, 0:128], (8, 128))
            right = jnp.broadcast_to(recv[i, at : at + 1, 128:256], (8, 128))
            t = jnp.where(tile_sub < 4, left, right)
            t = jnp.where(tile_lane // COLS == tile_sub % 4, t, 0.0)
            t = t + roll(t, 32, 1)
            t = t + roll(t, 64, 1)
            for h in range(2):
                gain[i, h * WIN + 4 + 8 * half : h * WIN + 12 + 8 * half, :] = t
        return carry

    lax.fori_loop(0, BLOCKS, unpack, 0, unroll=UNROLL)

    def around(i):
        gx, gy = i // 4, i % 4
        return (
            ((gx + 1) % 4) * 4 + gy,
            ((gx + 3) % 4) * 4 + gy,
            gx * 4 + (gy + 1) % 4,
            gx * 4 + (gy + 3) % 4,
        )

    def neighbours(ref, i, step):
        next_x, last_x, next_y, last_y = around(i)
        c = ref[i]
        dx, dy = SY * step, step
        total = jnp.where(x_at < SX - step, roll(c, -dx, 1), roll(ref[next_x], COLS - dx, 1))
        total += jnp.where(x_at >= step, roll(c, dx, 1), roll(ref[last_x], dx - COLS, 1))
        total += jnp.where(y_at < SY - step, roll(c, -dy, 1), roll(ref[next_y], SY - dy, 1))
        total += jnp.where(y_at >= step, roll(c, dy, 1), roll(ref[last_y], dy - SY, 1))
        return total + roll(c, step, 0) + roll(c, -step, 0)

    def restrict(i, carry):
        r = (1.0 - damping) * src[i] + (damping / fine_diag) * neighbours(src, i, 1)
        r = r + jnp.where(x_at % 2 == 0, roll(r, -SY, 1), roll(r, SY, 1))
        r = r + jnp.where(y_at % 2 == 0, roll(r, -1, 1), roll(r, 1, 1))
        r = r + jnp.where(z_odd == 0, roll(r, -1, 0), roll(r, 1, 0))
        coarse[i] = 0.125 * r
        return carry

    def correct(i, carry):
        two = 0.48 * coarse[i] + 0.04 * neighbours(coarse, i, 2)
        fine[i] = (damping / fine_diag) * src[i] + two
        return carry

    def smooth(i):
        y = (1.0 - damping) * fine[i] + (damping / fine_diag) * (src[i] + neighbours(fine, i, 1))
        return jnp.where(is_field, y, src[i])

    def mix(i, carry):
        field = smooth(i)
        first[i] = gain[i] * field
        parts = (field[0:WIN], field[WIN : 2 * WIN])
        here = lane[0:WIN]
        sums = [0.0, 0.0]
        for b in range(4):
            turned = [roll(p, -COLS * b, 1) for p in parts]
            near = here < 128 - COLS * b
            same = [
                jnp.where(near, turned[0], turned[1]),
                jnp.where(near, turned[1], turned[0]),
            ]
            for h in range(2):
                lanes = slice(h * 128, (h + 1) * 128)
                sums[h] = (
                    sums[h]
                    + coef[b : b + 1, lanes] * same[h]
                    + coef[4 + b : 5 + b, lanes] * same[1 - h]
                )
        for h in range(2):
            rows = slice(h * WIN, (h + 1) * WIN)
            coarse[i, rows, :] = gain[i, rows, :] * sums[h] + extra[i, rows, :]
        return carry

    def swap(i, carry):
        src[i] = coarse[i]
        return carry

    lax.fori_loop(0, BLOCKS, restrict, 0, unroll=UNROLL)
    lax.fori_loop(0, BLOCKS, correct, 0, unroll=UNROLL)
    lax.fori_loop(0, BLOCKS, mix, 0, unroll=UNROLL)
    lax.fori_loop(0, BLOCKS, swap, 0, unroll=UNROLL)
    lax.fori_loop(0, BLOCKS, restrict, 0, unroll=UNROLL)
    own = place[0]
    next_x, last_x, next_y, last_y = around(own)
    for i in (own, next_x, last_x, next_y, last_y):
        correct(i, 0)
    second = gain[own] * smooth(own)
    side_x = jnp.where(x_at < 2, roll(first[last_x], -16, 1), roll(first[next_x], 16, 1))
    side_y = jnp.where(y_at < 4, first[next_y], first[last_y])
    pieces = ((first[own], side_x), (side_y, second))
    for k in range(2):
        for m in range(2):
            for h in range(2):
                at = (2 * m + h) * 128
                coarse[0] = pieces[k][m]
                msg[4 * k : 4 * k + 4, at : at + 128] = coarse[0, h * WIN + 10 : h * WIN + 14, :]
    for j in range(out.shape[0]):
        out[j] = msg[...]


def last_kernel(table, recv, g, low, high, north, south, fluid, out, turn, fields):
    for j in range(recv.shape[0]):
        turn[4 * j : 4 * j + 4, 0:512] = recv[j, 0:4, :]
        turn[4 * j : 4 * j + 4, 512:1024] = recv[j, 4:8, :]
    for k in range(8):
        block = turn[:, k * 128 : (k + 1) * 128].T
        for r in range(4):
            for x in range(SX):
                at = (r * SX + x) * SY
                fields[k // 2, (k % 2) * 4 + r, x] = block[at : at + SY]
    sub = iota((SY, NZ), 0)

    def step(v, carry):
        psi = [table[ROWS + r, v] for r in range(ROWS)]

        def lift(part, x):
            total = psi[0] * fields[part, 0, x]
            for r in range(1, ROWS):
                total += psi[r] * fields[part, r, x]
            return total

        above, below = north[v], south[v]
        tiles = [lift(1, x) + low[v, x] for x in range(2)]
        tiles += [lift(0, x) + g[v, x] for x in range(SX)]
        tiles += [lift(1, 2 + x) + high[v, x] for x in range(2)]
        edges = [lift(2, x) + row_halo(above, below, x, sub) for x in range(SX)]
        moved = transport(table, v, tiles, edges, sub)
        for x in range(SX):
            out[v, x] = fluid[x] * moved[x] + lift(3, x)
        return carry

    lax.fori_loop(0, out.shape[0], step, 0)


VMEM = pltpu.MemorySpace.VMEM
SMEM = pltpu.MemorySpace.SMEM


def call(kernel, spaces, outs, scratch):
    specs = [pl.BlockSpec(memory_space=s) for s in spaces]
    shapes = [jax.ShapeDtypeStruct(s, F32) for s in outs]
    return pl.pallas_call(
        kernel,
        in_specs=specs,
        out_specs=[pl.BlockSpec(memory_space=VMEM) for _ in outs],
        out_shape=shapes,
        scratch_shapes=[pltpu.VMEM(s, F32) for s in scratch],
        interpret=INTERPRET,
        name=kernel.__name__,
    )


def stage_first(f, table, members):
    vels = f.shape[0]
    return call(
        first_kernel,
        (SMEM, VMEM),
        ((members, WIN, LANES), (vels, SY, NZ), (vels, SY, NZ)),
        ((LANES, NZ), (168, LANES)),
    )(table, f)


def stage_second(f, table, low, high, north, south, fluid, cross, members):
    vels = f.shape[0]
    return call(
        second_kernel,
        (SMEM,) + (VMEM,) * 7,
        (f.shape, (members, WIN2, LANES), (vels, SY, NZ), (vels, SY, NZ)),
        ((LANES, NZ), (168, LANES)),
    )(table, f, low, high, north, south, fluid, cross)


def wall_rows(cell_type, member):
    gain = jnp.where(cell_type == 1, 1.0, 0.5).astype(F32).reshape(COLS, NZ).T
    wrapped = jnp.concatenate([gain[NZ - 8 :], gain, gain[:16]], axis=0)
    return lax.dynamic_slice_in_dim(wrapped, 4 * member + 2, WIN2, axis=0).reshape(2, LANES)


def stage_middle(got_one, got_two, walls):
    one = jnp.sum(got_one, axis=0)
    two = jnp.sum(got_two, axis=0)
    whole = jnp.concatenate([one, walls[0:1], two[1 : WIN2 - 1], walls[1:2]], axis=0)
    cross = two[0].reshape(ROWS, COLS)[:, :ROWS]
    pick = np.zeros((ROWS, ROWS, ROWS), np.float32)
    for k in range(ROWS):
        for r in range(ROWS):
            pick[k, r, (r + k) % ROWS] = 1.0
    coef = jnp.sum(jnp.asarray(pick) * cross[None], axis=2)
    coef = jnp.broadcast_to(coef[:, :, None], (ROWS, ROWS, COLS)).reshape(ROWS, LANES)
    return jnp.broadcast_to(whole[None], (BLOCKS,) + whole.shape), coef


def stage_solve(place, got, coef, members):
    big = (BLOCKS, 2 * WIN, 128)
    return call(
        solve_kernel,
        (SMEM, VMEM, VMEM),
        ((members, 8, 512),),
        (big,) * 6 + ((8, 512),),
    )(place, got, coef)[0]


def stage_last(table, got, g, low, high, north, south, fluid):
    return call(
        last_kernel,
        (SMEM,) + (VMEM,) * 7,
        (g.shape,),
        ((NZ, 1024), (4, ROWS, SX, SY, NZ)),
    )(table, got, g, low, high, north, south, fluid)[0]


def halos(f, north, south):
    def ring(axis, step):
        count = lax.axis_size(axis)
        return [(i, (i + step) % count) for i in range(count)]

    low = lax.ppermute(f[:, SX - 2 :], "gx", ring("gx", 1))
    high = lax.ppermute(f[:, :2], "gx", ring("gx", -1))
    above = lax.ppermute(north, "gy", ring("gy", -1))
    below = lax.ppermute(south, "gy", ring("gy", 1))
    return low, high, above, below


def swap_all(x, axis):
    return lax.all_to_all(x, axis, 0, 0, tiled=True)


def local(f, vel_index, signs, cell_type, coupling):
    members = lax.axis_size("vert")
    table, cross = velocity_tables(vel_index, signs, coupling)
    fluid = jnp.where(cell_type == 1, 0.0, 1.0).astype(F32)
    walls = wall_rows(cell_type, lax.axis_index("vert"))
    place = (lax.axis_index("gx") * 4 + lax.axis_index("gy")).astype(jnp.int32).reshape(1)
    win_one, north, south = stage_first(f, table, members)
    got_one = swap_all(win_one, "vert")
    near, got_one = lax.optimization_barrier((halos(f, north, south), got_one))
    g, win_two, north, south = stage_second(f, table, *near, fluid, cross, members)
    got_two = swap_all(win_two, "vert")
    near, got_two = lax.optimization_barrier((halos(g, north, south), got_two))
    whole, coef = stage_middle(got_one, got_two, walls)
    got = swap_all(whole, ("gx", "gy"))
    sent = stage_solve(place, got, coef, members)
    got = swap_all(sent, "vert")
    return stage_last(table, got, g, *near, fluid)


def solution(mesh):
    in_specs = (
        P("vert", "gx", "gy", None),
        P(None, "vert"),
        P(None, "vert"),
        P("gx", "gy", None),
        P(),
    )
    out_specs = P("vert", "gx", "gy", None)
    return jax.shard_map(local, mesh=mesh, in_specs=in_specs, out_specs=out_specs, check_vma=False)
```

```python
import jax
import jax.numpy as jnp
import numpy as np
from jax import lax
from jax.experimental import pallas as pl
from jax.experimental.pallas import tpu as pltpu
from jax.sharding import Mesh
from jax.sharding import PartitionSpec as P


V = 1024
INTERPRET = False
UNROLL = 16

absorb = 0.5
damping = 0.8
fine_diag = 6.5
prandtl = 2.0 / 3.0

SX, SY, NZ = 4, 8, 128
COLS = SX * SY
ROWS = 8
LANES = ROWS * COLS
BLOCKS = 16
WIN = 24
WIN2 = 16
F32 = jnp.float32


def roll(x, shift, axis):
    return pltpu.roll(x, shift % x.shape[axis], axis)


def iota(shape, dim):
    return lax.broadcasted_iota(jnp.int32, shape, dim)


def velocity_tables(vel_index, signs, coupling):
    speeds = (vel_index.astype(F32) + 0.5) * 0.25
    positive = signs.astype(F32)
    veloc = speeds * (positive * 2.0 - 1.0)
    square = jnp.sum(veloc * veloc, axis=0)
    weight = 64.0 * jnp.exp(-square) / V
    vel_x, vel_y, vel_z = (veloc[0], veloc[1], veloc[2])
    unit_row = jnp.ones_like(vel_x)
    heat_term = square - 2.5
    basis = (
        jnp.stack(
            [
                unit_row,
                vel_x,
                vel_y,
                vel_z,
                square - 1.5,
                vel_x * vel_y,
                vel_x * vel_z,
                vel_y * vel_z,
                vel_x * vel_x - vel_y * vel_y,
                vel_y * vel_y - vel_z * vel_z,
                heat_term * vel_x,
                heat_term * vel_y,
                heat_term * vel_z,
            ]
        )
        * weight[None]
    )
    shakhov = 0.8 * (1.0 - prandtl)
    equil = jnp.stack(
        [
            unit_row,
            2.0 * vel_x,
            2.0 * vel_y,
            2.0 * vel_z,
            2.0 / 3.0 * (square - 1.5),
            shakhov * heat_term * vel_x,
            shakhov * heat_term * vel_y,
            shakhov * heat_term * vel_z,
        ]
    )
    mixed = jnp.sum(coupling[:, :, None] * basis[None, 5:13], axis=1)
    source_basis = jnp.concatenate([absorb * basis[0:5] + mixed, basis[10:13]], axis=0)
    centre = 0.5 - 0.3 * jnp.sum(speeds, axis=0)
    table = jnp.concatenate(
        [
            source_basis,
            equil,
            centre[None],
            0.4 * speeds * positive,
            0.4 * speeds * (1.0 - positive),
            jnp.zeros_like(centre)[None],
        ],
        axis=0,
    )
    cross = jnp.sum(source_basis[:, None] * equil[None], axis=2)
    cross_row = jnp.pad(cross, ((0, 0), (0, COLS - ROWS))).reshape(1, LANES)
    return table, cross_row


def moments(src, table, m_scr, ext):
    zero = jnp.zeros((SY, NZ), F32)

    def step(v, accs):
        tiles = [src[v, x] for x in range(SX)]
        out = []
        for r in range(ROWS):
            w = table[r, v]
            out += [accs[r * SX + x] + w * tiles[x] for x in range(SX)]
        return tuple(out)

    accs = lax.fori_loop(0, src.shape[0], step, (zero,) * (ROWS * SX), unroll=2)
    for i, acc in enumerate(accs):
        m_scr[i * SY : (i + 1) * SY, :] = acc
    for h in range(2):
        turned = m_scr[h * 128 : (h + 1) * 128, :].T
        lanes = slice(h * 128, (h + 1) * 128)
        ext[16:144, lanes] = turned
        ext[0:16, lanes] = turned[112:128]
        ext[144:168, lanes] = turned[0:24]


def first_kernel(table, f, win, north, south, m_scr, ext):
    moments(f, table, m_scr, ext)
    for j in range(win.shape[0]):
        win[j] = ext[4 * j + 6 : 4 * j + 6 + WIN, :]
    pack_rows(f, north, south)


def pack_rows(src, north, south):
    pair = iota((SY, NZ), 0) // 2

    def step(v, carry):
        top = roll(src[v, 0], 0, 0)
        low = roll(src[v, 0], -6, 0)
        for x in range(1, SX):
            tile = src[v, x]
            top = jnp.where(pair == x, roll(tile, 2 * x, 0), top)
            low = jnp.where(pair == x, roll(tile, 2 * x - 6, 0), low)
        north[v] = top
        south[v] = low
        return carry

    lax.fori_loop(0, src.shape[0], step, 0, unroll=4)


def row_halo(north, south, x, sub):
    return jnp.where(sub < 4, roll(north, -2 * x, 0), roll(south, 6 - 2 * x, 0))


def transport(table, v, tiles, edges, sub):
    centre = table[16, v]
    up = [table[17 + d, v] for d in range(3)]
    down = [table[20 + d, v] for d in range(3)]
    out = []
    for x in range(SX):
        f = tiles[x + 2]
        e = edges[x]
        acc = centre * f
        acc += up[0] * (tiles[x + 1] - 0.25 * tiles[x])
        acc += down[0] * (tiles[x + 3] - 0.25 * tiles[x + 4])
        back_one = roll(jnp.where(sub >= 7, e, f), 1, 0)
        back_two = roll(jnp.where(sub >= 6, e, f), 2, 0)
        front_one = roll(jnp.where(sub < 1, e, f), -1, 0)
        front_two = roll(jnp.where(sub < 2, e, f), -2, 0)
        acc += up[1] * (back_one - 0.25 * back_two)
        acc += down[1] * (front_one - 0.25 * front_two)
        acc += up[2] * (roll(f, 1, 1) - 0.25 * roll(f, 2, 1))
        acc += down[2] * (roll(f, -1, 1) - 0.25 * roll(f, -2, 1))
        out.append(acc)
    return out


def second_kernel(table, f, low, high, north, south, fluid, cross, g, win, g_north, g_south, m_scr, ext):
    sub = iota((SY, NZ), 0)

    def step(v, carry):
        tiles = [low[v, 0], low[v, 1]] + [f[v, x] for x in range(SX)] + [high[v, 0], high[v, 1]]
        above, below = north[v], south[v]
        edges = [row_halo(above, below, x, sub) for x in range(SX)]
        moved = transport(table, v, tiles, edges, sub)
        for x in range(SX):
            g[v, x] = fluid[x] * moved[x]
        return carry

    lax.fori_loop(0, f.shape[0], step, 0, unroll=2)
    moments(g, table, m_scr, ext)
    for j in range(win.shape[0]):
        win[j] = ext[4 * j + 10 : 4 * j + 10 + WIN2, :]
        win[j, 0:1, :] = cross[...]
    pack_rows(g, g_north, g_south)


def solve_kernel(place, near, far, coef, out, src, coarse, fine, gain, extra, first, msg):
    shape = (2 * WIN, 128)
    lane = iota(shape, 1)
    x_at = (lane // SY) % SX
    y_at = lane % SY
    z_odd = iota(shape, 0) % 2
    is_field = (iota(shape, 0) // WIN) * 4 + lane // COLS < 5
    tile_sub = iota((8, 128), 0)
    tile_lane = iota((8, 128), 1)

    def unpack(i, carry):
        mine = i % 2 == place[1]
        rows = jnp.where(mine, near[i // 2], far[i // 2])
        for h in range(2):
            lanes = slice(h * 128, (h + 1) * 128)
            src[i, h * WIN : (h + 1) * WIN, :] = rows[0:WIN, lanes]
            extra[i, h * WIN : h * WIN + 4, :] = jnp.zeros((4, 128), F32)
            extra[i, h * WIN + 20 : (h + 1) * WIN, :] = jnp.zeros((4, 128), F32)
            extra[i, h * WIN + 4 : h * WIN + 20, :] = rows[WIN : WIN + WIN2, lanes]
        gain[i] = jnp.zeros(shape, F32)
        for half, at in enumerate((WIN, WIN + WIN2 - 1)):
            left = jnp.broadcast_to(rows[at : at + 1, 0:128], (8, 128))
            right = jnp.broadcast_to(rows[at : at + 1, 128:256], (8, 128))
            t = jnp.where(tile_sub < 4, left, right)
            t = jnp.where(tile_lane // COLS == tile_sub % 4, t, 0.0)
            t = t + roll(t, 32, 1)
            t = t + roll(t, 64, 1)
            for h in range(2):
                gain[i, h * WIN + 4 + 8 * half : h * WIN + 12 + 8 * half, :] = t
        return carry

    lax.fori_loop(0, BLOCKS, unpack, 0, unroll=UNROLL)

    def around(i):
        gx, gy = i // 4, i % 4
        return (
            ((gx + 1) % 4) * 4 + gy,
            ((gx + 3) % 4) * 4 + gy,
            gx * 4 + (gy + 1) % 4,
            gx * 4 + (gy + 3) % 4,
        )

    def neighbours(ref, i, step):
        next_x, last_x, next_y, last_y = around(i)
        c = ref[i]
        dx, dy = SY * step, step
        total = jnp.where(x_at < SX - step, roll(c, -dx, 1), roll(ref[next_x], COLS - dx, 1))
        total += jnp.where(x_at >= step, roll(c, dx, 1), roll(ref[last_x], dx - COLS, 1))
        total += jnp.where(y_at < SY - step, roll(c, -dy, 1), roll(ref[next_y], SY - dy, 1))
        total += jnp.where(y_at >= step, roll(c, dy, 1), roll(ref[last_y], dy - SY, 1))
        return total + roll(c, step, 0) + roll(c, -step, 0)

    def restrict(i, carry):
        r = (1.0 - damping) * src[i] + (damping / fine_diag) * neighbours(src, i, 1)
        r = r + jnp.where(x_at % 2 == 0, roll(r, -SY, 1), roll(r, SY, 1))
        r = r + jnp.where(y_at % 2 == 0, roll(r, -1, 1), roll(r, 1, 1))
        r = r + jnp.where(z_odd == 0, roll(r, -1, 0), roll(r, 1, 0))
        coarse[i] = 0.125 * r
        return carry

    def correct(i, carry):
        two = 0.48 * coarse[i] + 0.04 * neighbours(coarse, i, 2)
        fine[i] = (damping / fine_diag) * src[i] + two
        return carry

    def smooth(i):
        y = (1.0 - damping) * fine[i] + (damping / fine_diag) * (src[i] + neighbours(fine, i, 1))
        return jnp.where(is_field, y, src[i])

    def mix(i, carry):
        field = smooth(i)
        first[i] = gain[i] * field
        parts = (field[0:WIN], field[WIN : 2 * WIN])
        here = lane[0:WIN]
        sums = [0.0, 0.0]
        for b in range(4):
            turned = [roll(p, -COLS * b, 1) for p in parts]
            near = here < 128 - COLS * b
            same = [
                jnp.where(near, turned[0], turned[1]),
                jnp.where(near, turned[1], turned[0]),
            ]
            for h in range(2):
                lanes = slice(h * 128, (h + 1) * 128)
                sums[h] = (
                    sums[h]
                    + coef[b : b + 1, lanes] * same[h]
                    + coef[4 + b : 5 + b, lanes] * same[1 - h]
                )
        for h in range(2):
            rows = slice(h * WIN, (h + 1) * WIN)
            coarse[i, rows, :] = gain[i, rows, :] * sums[h] + extra[i, rows, :]
        return carry

    def swap(i, carry):
        src[i] = coarse[i]
        return carry

    lax.fori_loop(0, BLOCKS, restrict, 0, unroll=UNROLL)
    lax.fori_loop(0, BLOCKS, correct, 0, unroll=UNROLL)
    lax.fori_loop(0, BLOCKS, mix, 0, unroll=UNROLL)
    lax.fori_loop(0, BLOCKS, swap, 0, unroll=UNROLL)
    lax.fori_loop(0, BLOCKS, restrict, 0, unroll=UNROLL)
    own = place[0]
    next_x, last_x, next_y, last_y = around(own)
    for i in (own, next_x, last_x, next_y, last_y):
        correct(i, 0)
    second = gain[own] * smooth(own)
    side_x = jnp.where(x_at < 2, roll(first[last_x], -16, 1), roll(first[next_x], 16, 1))
    side_y = jnp.where(y_at < 4, first[next_y], first[last_y])
    pieces = ((first[own], side_x), (side_y, second))
    for k in range(2):
        for m in range(2):
            for h in range(2):
                at = (2 * m + h) * 128
                coarse[0] = pieces[k][m]
                msg[4 * k : 4 * k + 4, at : at + 128] = coarse[0, h * WIN + 10 : h * WIN + 14, :]
    for j in range(out.shape[0]):
        out[j] = msg[...]


def last_kernel(table, recv, g, low, high, north, south, fluid, out, turn, fields):
    for j in range(recv.shape[0]):
        turn[4 * j : 4 * j + 4, 0:512] = recv[j, 0:4, :]
        turn[4 * j : 4 * j + 4, 512:1024] = recv[j, 4:8, :]
    for k in range(8):
        block = turn[:, k * 128 : (k + 1) * 128].T
        for r in range(4):
            for x in range(SX):
                at = (r * SX + x) * SY
                fields[k // 2, (k % 2) * 4 + r, x] = block[at : at + SY]
    sub = iota((SY, NZ), 0)

    def step(v, carry):
        psi = [table[ROWS + r, v] for r in range(ROWS)]

        def lift(part, x):
            total = psi[0] * fields[part, 0, x]
            for r in range(1, ROWS):
                total += psi[r] * fields[part, r, x]
            return total

        above, below = north[v], south[v]
        tiles = [lift(1, x) + low[v, x] for x in range(2)]
        tiles += [lift(0, x) + g[v, x] for x in range(SX)]
        tiles += [lift(1, 2 + x) + high[v, x] for x in range(2)]
        edges = [lift(2, x) + row_halo(above, below, x, sub) for x in range(SX)]
        moved = transport(table, v, tiles, edges, sub)
        for x in range(SX):
            out[v, x] = fluid[x] * moved[x] + lift(3, x)
        return carry

    lax.fori_loop(0, out.shape[0], step, 0)


GY = ("zh", "core")
VMEM = pltpu.MemorySpace.VMEM
SMEM = pltpu.MemorySpace.SMEM


def call(kernel, spaces, outs, scratch):
    specs = [pl.BlockSpec(memory_space=s) for s in spaces]
    shapes = [jax.ShapeDtypeStruct(s, F32) for s in outs]
    return pl.pallas_call(
        kernel,
        in_specs=specs,
        out_specs=[pl.BlockSpec(memory_space=VMEM) for _ in outs],
        out_shape=shapes,
        scratch_shapes=[pltpu.VMEM(s, F32) for s in scratch],
        interpret=INTERPRET,
    )


def stage_first(f, table, members):
    vels = f.shape[0]
    return call(
        first_kernel,
        (SMEM, VMEM),
        ((members, WIN, LANES), (vels, SY, NZ), (vels, SY, NZ)),
        ((LANES, NZ), (168, LANES)),
    )(table, f)


def stage_second(f, table, low, high, north, south, fluid, cross, members):
    vels = f.shape[0]
    return call(
        second_kernel,
        (SMEM,) + (VMEM,) * 7,
        (f.shape, (members, WIN2, LANES), (vels, SY, NZ), (vels, SY, NZ)),
        ((LANES, NZ), (168, LANES)),
    )(table, f, low, high, north, south, fluid, cross)


def wall_rows(cell_type, member):
    gain = jnp.where(cell_type == 1, 1.0, 0.5).astype(F32).reshape(COLS, NZ).T
    wrapped = jnp.concatenate([gain[NZ - 8 :], gain, gain[:16]], axis=0)
    return lax.dynamic_slice_in_dim(wrapped, 4 * member + 2, WIN2, axis=0).reshape(2, LANES)


def stage_middle(got_one, got_two, walls):
    one = jnp.sum(got_one, axis=0)
    two = jnp.sum(got_two, axis=0)
    whole = jnp.concatenate([one, walls[0:1], two[1 : WIN2 - 1], walls[1:2]], axis=0)
    cross = two[0].reshape(ROWS, COLS)[:, :ROWS]
    pick = np.zeros((ROWS, ROWS, ROWS), np.float32)
    for k in range(ROWS):
        for r in range(ROWS):
            pick[k, r, (r + k) % ROWS] = 1.0
    coef = jnp.sum(jnp.asarray(pick) * cross[None], axis=2)
    coef = jnp.broadcast_to(coef[:, :, None], (ROWS, ROWS, COLS)).reshape(ROWS, LANES)
    return jnp.broadcast_to(whole[None], (BLOCKS // 2,) + whole.shape), coef


def stage_solve(place, near, far, coef, members):
    big = (BLOCKS, 2 * WIN, 128)
    return call(
        solve_kernel,
        (SMEM, VMEM, VMEM, VMEM),
        ((members, 8, 512),),
        (big,) * 6 + ((8, 512),),
    )(place, near, far, coef)[0]


def stage_last(table, got, g, low, high, north, south, fluid):
    return call(
        last_kernel,
        (SMEM,) + (VMEM,) * 7,
        (g.shape,),
        ((NZ, 1024), (4, ROWS, SX, SY, NZ)),
    )(table, got, g, low, high, north, south, fluid)[0]


def halos(f, north, south):
    def ring(axis, step):
        count = lax.axis_size(axis)
        return [(i, (i + step) % count) for i in range(count)]

    low = lax.ppermute(f[:, SX - 2 :], "gx", ring("gx", 1))
    high = lax.ppermute(f[:, :2], "gx", ring("gx", -1))
    above = lax.ppermute(north, GY, ring(GY, -1))
    below = lax.ppermute(south, GY, ring(GY, 1))
    return low, high, above, below


def swap_all(x, axis):
    return lax.all_to_all(x, axis, 0, 0, tiled=True)


def local(f, vel_index, signs, cell_type, coupling):
    members = lax.axis_size("vert")
    table, cross = velocity_tables(vel_index, signs, coupling)
    fluid = jnp.where(cell_type == 1, 0.0, 1.0).astype(F32)
    walls = wall_rows(cell_type, lax.axis_index("vert"))
    own = lax.axis_index("gx") * 4 + lax.axis_index(GY)
    place = jnp.stack([own, lax.axis_index("core")]).astype(jnp.int32)
    win_one, north, south = stage_first(f, table, members)
    got_one = swap_all(win_one, "vert")
    near = halos(f, north, south)
    near, got_one = lax.optimization_barrier((near, got_one))
    g, win_two, north, south = stage_second(f, table, *near, fluid, cross, members)
    got_two = swap_all(win_two, "vert")
    near = halos(g, north, south)
    whole, coef = stage_middle(got_one, got_two, walls)
    this_core = swap_all(whole, ("gx", "zh"))
    that_core = lax.ppermute(this_core, "core", [(0, 1), (1, 0)])
    sent = stage_solve(place, this_core, that_core, coef, members)
    got = swap_all(sent, "vert")
    return stage_last(table, got, g, *near, fluid)


def solution(mesh):
    in_specs = (
        P("vert", "gx", GY, None),
        P(None, "vert"),
        P(None, "vert"),
        P("gx", GY, None),
        P(),
    )
    out_specs = P("vert", "gx", GY, None)
    fine_mesh = Mesh(mesh.devices.reshape(4, 2, 2, -1), ("gx",) + GY + ("vert",))
    return jax.shard_map(
        local, mesh=fine_mesh, in_specs=in_specs, out_specs=out_specs, check_vma=False
    )
```

```python
import jax
import jax.numpy as jnp
import numpy as np
from jax import lax
from jax.experimental import pallas as pl
from jax.experimental.pallas import tpu as pltpu
from jax.sharding import Mesh
from jax.sharding import PartitionSpec as P


V = 1024
INTERPRET = False
UNROLL = 16
LAST, SECOND, MOMENTS = 2, 8, 8

absorb = 0.5
damping = 0.8
fine_diag = 6.5
prandtl = 2.0 / 3.0

SX, SY, NZ = 4, 8, 128
COLS = SX * SY
ROWS = 8
LANES = ROWS * COLS
BLOCKS = 16
WIN = 24
WIN2 = 16
F32 = jnp.float32


def roll(x, shift, axis):
    return pltpu.roll(x, shift % x.shape[axis], axis)


def iota(shape, dim):
    return lax.broadcasted_iota(jnp.int32, shape, dim)


def velocity_tables(vel_index, signs, coupling):
    speeds = (vel_index.astype(F32) + 0.5) * 0.25
    positive = signs.astype(F32)
    veloc = speeds * (positive * 2.0 - 1.0)
    square = jnp.sum(veloc * veloc, axis=0)
    weight = 64.0 * jnp.exp(-square) / V
    vel_x, vel_y, vel_z = (veloc[0], veloc[1], veloc[2])
    unit_row = jnp.ones_like(vel_x)
    heat_term = square - 2.5
    basis = (
        jnp.stack(
            [
                unit_row,
                vel_x,
                vel_y,
                vel_z,
                square - 1.5,
                vel_x * vel_y,
                vel_x * vel_z,
                vel_y * vel_z,
                vel_x * vel_x - vel_y * vel_y,
                vel_y * vel_y - vel_z * vel_z,
                heat_term * vel_x,
                heat_term * vel_y,
                heat_term * vel_z,
            ]
        )
        * weight[None]
    )
    shakhov = 0.8 * (1.0 - prandtl)
    equil = jnp.stack(
        [
            unit_row,
            2.0 * vel_x,
            2.0 * vel_y,
            2.0 * vel_z,
            2.0 / 3.0 * (square - 1.5),
            shakhov * heat_term * vel_x,
            shakhov * heat_term * vel_y,
            shakhov * heat_term * vel_z,
        ]
    )
    mixed = jnp.sum(coupling[:, :, None] * basis[None, 5:13], axis=1)
    source_basis = jnp.concatenate([absorb * basis[0:5] + mixed, basis[10:13]], axis=0)
    centre = 0.5 - 0.3 * jnp.sum(speeds, axis=0)
    table = jnp.concatenate(
        [
            source_basis,
            equil,
            centre[None],
            0.4 * speeds * positive,
            0.4 * speeds * (1.0 - positive),
            jnp.zeros_like(centre)[None],
        ],
        axis=0,
    )
    cross = jnp.sum(source_basis[:, None] * equil[None], axis=2)
    cross_row = jnp.pad(cross, ((0, 0), (0, COLS - ROWS))).reshape(1, LANES)
    return table, cross_row


def moments(src, table, m_scr, ext):
    zero = jnp.zeros((SY, NZ), F32)

    def step(v, accs):
        tiles = [src[v, x] for x in range(SX)]
        out = []
        for r in range(ROWS):
            w = table[r, v]
            out += [accs[r * SX + x] + w * tiles[x] for x in range(SX)]
        return tuple(out)

    accs = lax.fori_loop(0, src.shape[0], step, (zero,) * (ROWS * SX), unroll=MOMENTS)
    for i, acc in enumerate(accs):
        m_scr[i * SY : (i + 1) * SY, :] = acc
    for h in range(2):
        turned = m_scr[h * 128 : (h + 1) * 128, :].T
        lanes = slice(h * 128, (h + 1) * 128)
        ext[16:144, lanes] = turned
        ext[0:16, lanes] = turned[112:128]
        ext[144:168, lanes] = turned[0:24]


def first_kernel(table, f, win, north, south, m_scr, ext):
    moments(f, table, m_scr, ext)
    for j in range(win.shape[0]):
        win[j] = ext[4 * j + 6 : 4 * j + 6 + WIN, :]
    pack_rows(f, north, south)


def pack_rows(src, north, south):
    pair = iota((SY, NZ), 0) // 2

    def step(v, carry):
        top = roll(src[v, 0], 0, 0)
        low = roll(src[v, 0], -6, 0)
        for x in range(1, SX):
            tile = src[v, x]
            top = jnp.where(pair == x, roll(tile, 2 * x, 0), top)
            low = jnp.where(pair == x, roll(tile, 2 * x - 6, 0), low)
        north[v] = top
        south[v] = low
        return carry

    lax.fori_loop(0, src.shape[0], step, 0, unroll=4)


def row_halo(north, south, x, sub):
    return jnp.where(sub < 4, roll(north, -2 * x, 0), roll(south, 6 - 2 * x, 0))


def transport(table, v, tiles, edges, sub):
    centre = table[16, v]
    up = [table[17 + d, v] for d in range(3)]
    down = [table[20 + d, v] for d in range(3)]
    out = []
    for x in range(SX):
        f = tiles[x + 2]
        e = edges[x]
        acc = centre * f
        acc += up[0] * (tiles[x + 1] - 0.25 * tiles[x])
        acc += down[0] * (tiles[x + 3] - 0.25 * tiles[x + 4])
        back_one = roll(jnp.where(sub >= 7, e, f), 1, 0)
        back_two = roll(jnp.where(sub >= 6, e, f), 2, 0)
        front_one = roll(jnp.where(sub < 1, e, f), -1, 0)
        front_two = roll(jnp.where(sub < 2, e, f), -2, 0)
        acc += up[1] * (back_one - 0.25 * back_two)
        acc += down[1] * (front_one - 0.25 * front_two)
        acc += up[2] * (roll(f, 1, 1) - 0.25 * roll(f, 2, 1))
        acc += down[2] * (roll(f, -1, 1) - 0.25 * roll(f, -2, 1))
        out.append(acc)
    return out


def second_kernel(table, f, low, high, north, south, fluid, cross, g, win, g_north, g_south, m_scr, ext):
    sub = iota((SY, NZ), 0)

    def step(v, carry):
        tiles = [low[v, 0], low[v, 1]] + [f[v, x] for x in range(SX)] + [high[v, 0], high[v, 1]]
        above, below = north[v], south[v]
        edges = [row_halo(above, below, x, sub) for x in range(SX)]
        moved = transport(table, v, tiles, edges, sub)
        for x in range(SX):
            g[v, x] = fluid[x] * moved[x]
        return carry

    lax.fori_loop(0, f.shape[0], step, 0, unroll=SECOND)
    moments(g, table, m_scr, ext)
    for j in range(win.shape[0]):
        win[j] = ext[4 * j + 10 : 4 * j + 10 + WIN2, :]
        win[j, 0:1, :] = cross[...]
    pack_rows(g, g_north, g_south)


def solve_kernel(place, near, far, coef, out, src, coarse, fine, gain, extra, first, msg):
    shape = (2 * WIN, 128)
    lane = iota(shape, 1)
    x_at = (lane // SY) % SX
    y_at = lane % SY
    z_odd = iota(shape, 0) % 2
    is_field = (iota(shape, 0) // WIN) * 4 + lane // COLS < 5
    tile_sub = iota((8, 128), 0)
    tile_lane = iota((8, 128), 1)

    def unpack(i, carry):
        mine = i % 2 == place[1]
        rows = jnp.where(mine, near[i // 2], far[i // 2])
        for h in range(2):
            lanes = slice(h * 128, (h + 1) * 128)
            src[i, h * WIN : (h + 1) * WIN, :] = rows[0:WIN, lanes]
            extra[i, h * WIN : h * WIN + 4, :] = jnp.zeros((4, 128), F32)
            extra[i, h * WIN + 20 : (h + 1) * WIN, :] = jnp.zeros((4, 128), F32)
            extra[i, h * WIN + 4 : h * WIN + 20, :] = rows[WIN : WIN + WIN2, lanes]
        gain[i] = jnp.zeros(shape, F32)
        for half, at in enumerate((WIN, WIN + WIN2 - 1)):
            left = jnp.broadcast_to(rows[at : at + 1, 0:128], (8, 128))
            right = jnp.broadcast_to(rows[at : at + 1, 128:256], (8, 128))
            t = jnp.where(tile_sub < 4, left, right)
            t = jnp.where(tile_lane // COLS == tile_sub % 4, t, 0.0)
            t = t + roll(t, 32, 1)
            t = t + roll(t, 64, 1)
            for h in range(2):
                gain[i, h * WIN + 4 + 8 * half : h * WIN + 12 + 8 * half, :] = t
        return carry

    lax.fori_loop(0, BLOCKS, unpack, 0, unroll=UNROLL)

    def around(i):
        gx, gy = i // 4, i % 4
        return (
            ((gx + 1) % 4) * 4 + gy,
            ((gx + 3) % 4) * 4 + gy,
            gx * 4 + (gy + 1) % 4,
            gx * 4 + (gy + 3) % 4,
        )

    def neighbours(ref, i, step):
        next_x, last_x, next_y, last_y = around(i)
        c = ref[i]
        dx, dy = SY * step, step
        total = jnp.where(x_at < SX - step, roll(c, -dx, 1), roll(ref[next_x], COLS - dx, 1))
        total += jnp.where(x_at >= step, roll(c, dx, 1), roll(ref[last_x], dx - COLS, 1))
        total += jnp.where(y_at < SY - step, roll(c, -dy, 1), roll(ref[next_y], SY - dy, 1))
        total += jnp.where(y_at >= step, roll(c, dy, 1), roll(ref[last_y], dy - SY, 1))
        return total + roll(c, step, 0) + roll(c, -step, 0)

    def restrict(i, carry):
        r = (1.0 - damping) * src[i] + (damping / fine_diag) * neighbours(src, i, 1)
        r = r + jnp.where(x_at % 2 == 0, roll(r, -SY, 1), roll(r, SY, 1))
        r = r + jnp.where(y_at % 2 == 0, roll(r, -1, 1), roll(r, 1, 1))
        r = r + jnp.where(z_odd == 0, roll(r, -1, 0), roll(r, 1, 0))
        coarse[i] = 0.125 * r
        return carry

    def correct(i, carry):
        two = 0.48 * coarse[i] + 0.04 * neighbours(coarse, i, 2)
        fine[i] = (damping / fine_diag) * src[i] + two
        return carry

    def smooth(i):
        y = (1.0 - damping) * fine[i] + (damping / fine_diag) * (src[i] + neighbours(fine, i, 1))
        return jnp.where(is_field, y, src[i])

    def mix(i, carry):
        field = smooth(i)
        first[i] = gain[i] * field
        parts = (field[0:WIN], field[WIN : 2 * WIN])
        here = lane[0:WIN]
        sums = [0.0, 0.0]
        for b in range(4):
            turned = [roll(p, -COLS * b, 1) for p in parts]
            near = here < 128 - COLS * b
            same = [
                jnp.where(near, turned[0], turned[1]),
                jnp.where(near, turned[1], turned[0]),
            ]
            for h in range(2):
                lanes = slice(h * 128, (h + 1) * 128)
                sums[h] = (
                    sums[h]
                    + coef[b : b + 1, lanes] * same[h]
                    + coef[4 + b : 5 + b, lanes] * same[1 - h]
                )
        for h in range(2):
            rows = slice(h * WIN, (h + 1) * WIN)
            coarse[i, rows, :] = gain[i, rows, :] * sums[h] + extra[i, rows, :]
        return carry

    def swap(i, carry):
        src[i] = coarse[i]
        return carry

    lax.fori_loop(0, BLOCKS, restrict, 0, unroll=UNROLL)
    lax.fori_loop(0, BLOCKS, correct, 0, unroll=UNROLL)
    lax.fori_loop(0, BLOCKS, mix, 0, unroll=UNROLL)
    lax.fori_loop(0, BLOCKS, swap, 0, unroll=UNROLL)
    lax.fori_loop(0, BLOCKS, restrict, 0, unroll=UNROLL)
    own = place[0]
    next_x, last_x, next_y, last_y = around(own)
    for i in (own, next_x, last_x, next_y, last_y):
        correct(i, 0)
    second = gain[own] * smooth(own)
    side_x = jnp.where(x_at < 2, roll(first[last_x], -16, 1), roll(first[next_x], 16, 1))
    side_y = jnp.where(y_at < 4, first[next_y], first[last_y])
    pieces = ((first[own], side_x), (side_y, second))
    for k in range(2):
        for m in range(2):
            for h in range(2):
                at = (2 * m + h) * 128
                coarse[0] = pieces[k][m]
                msg[4 * k : 4 * k + 4, at : at + 128] = coarse[0, h * WIN + 10 : h * WIN + 14, :]
    for j in range(out.shape[0]):
        out[j] = msg[...]


def last_kernel(table, recv, g, low, high, north, south, fluid, out, turn, fields):
    for j in range(recv.shape[0]):
        turn[4 * j : 4 * j + 4, 0:512] = recv[j, 0:4, :]
        turn[4 * j : 4 * j + 4, 512:1024] = recv[j, 4:8, :]
    for k in range(8):
        block = turn[:, k * 128 : (k + 1) * 128].T
        for r in range(4):
            for x in range(SX):
                at = (r * SX + x) * SY
                fields[k // 2, (k % 2) * 4 + r, x] = block[at : at + SY]
    sub = iota((SY, NZ), 0)

    def step(v, carry):
        psi = [table[ROWS + r, v] for r in range(ROWS)]

        def lift(part, x):
            total = psi[0] * fields[part, 0, x]
            for r in range(1, ROWS):
                total += psi[r] * fields[part, r, x]
            return total

        above, below = north[v], south[v]
        tiles = [lift(1, x) + low[v, x] for x in range(2)]
        tiles += [lift(0, x) + g[v, x] for x in range(SX)]
        tiles += [lift(1, 2 + x) + high[v, x] for x in range(2)]
        edges = [lift(2, x) + row_halo(above, below, x, sub) for x in range(SX)]
        moved = transport(table, v, tiles, edges, sub)
        for x in range(SX):
            out[v, x] = fluid[x] * moved[x] + lift(3, x)
        return carry

    lax.fori_loop(0, out.shape[0], step, 0, unroll=LAST)


GY = ("zh", "core")
VMEM = pltpu.MemorySpace.VMEM
SMEM = pltpu.MemorySpace.SMEM


def call(kernel, spaces, outs, scratch):
    specs = [pl.BlockSpec(memory_space=s) for s in spaces]
    shapes = [jax.ShapeDtypeStruct(s, F32) for s in outs]
    return pl.pallas_call(
        kernel,
        in_specs=specs,
        out_specs=[pl.BlockSpec(memory_space=VMEM) for _ in outs],
        out_shape=shapes,
        scratch_shapes=[pltpu.VMEM(s, F32) for s in scratch],
        interpret=INTERPRET,
    )


def stage_first(f, table, members):
    vels = f.shape[0]
    return call(
        first_kernel,
        (SMEM, VMEM),
        ((members, WIN, LANES), (vels, SY, NZ), (vels, SY, NZ)),
        ((LANES, NZ), (168, LANES)),
    )(table, f)


def stage_second(f, table, low, high, north, south, fluid, cross, members):
    vels = f.shape[0]
    return call(
        second_kernel,
        (SMEM,) + (VMEM,) * 7,
        (f.shape, (members, WIN2, LANES), (vels, SY, NZ), (vels, SY, NZ)),
        ((LANES, NZ), (168, LANES)),
    )(table, f, low, high, north, south, fluid, cross)


def wall_rows(cell_type, member):
    gain = jnp.where(cell_type == 1, 1.0, 0.5).astype(F32).reshape(COLS, NZ).T
    wrapped = jnp.concatenate([gain[NZ - 8 :], gain, gain[:16]], axis=0)
    return lax.dynamic_slice_in_dim(wrapped, 4 * member + 2, WIN2, axis=0).reshape(2, LANES)


def stage_middle(got_one, got_two, walls):
    one = jnp.sum(got_one, axis=0)
    two = jnp.sum(got_two, axis=0)
    whole = jnp.concatenate([one, walls[0:1], two[1 : WIN2 - 1], walls[1:2]], axis=0)
    cross = two[0].reshape(ROWS, COLS)[:, :ROWS]
    pick = np.zeros((ROWS, ROWS, ROWS), np.float32)
    for k in range(ROWS):
        for r in range(ROWS):
            pick[k, r, (r + k) % ROWS] = 1.0
    coef = jnp.sum(jnp.asarray(pick) * cross[None], axis=2)
    coef = jnp.broadcast_to(coef[:, :, None], (ROWS, ROWS, COLS)).reshape(ROWS, LANES)
    return jnp.broadcast_to(whole[None], (BLOCKS // 2,) + whole.shape), coef


def stage_solve(place, near, far, coef, members):
    big = (BLOCKS, 2 * WIN, 128)
    return call(
        solve_kernel,
        (SMEM, VMEM, VMEM, VMEM),
        ((members, 8, 512),),
        (big,) * 6 + ((8, 512),),
    )(place, near, far, coef)[0]


def stage_last(table, got, g, low, high, north, south, fluid):
    return call(
        last_kernel,
        (SMEM,) + (VMEM,) * 7,
        (g.shape,),
        ((NZ, 1024), (4, ROWS, SX, SY, NZ)),
    )(table, got, g, low, high, north, south, fluid)[0]


def halos(f, north, south):
    def ring(axis, step):
        count = lax.axis_size(axis)
        return [(i, (i + step) % count) for i in range(count)]

    low = lax.ppermute(f[:, SX - 2 :], "gx", ring("gx", 1))
    high = lax.ppermute(f[:, :2], "gx", ring("gx", -1))
    above = lax.ppermute(north, GY, ring(GY, -1))
    below = lax.ppermute(south, GY, ring(GY, 1))
    return low, high, above, below


def swap_all(x, axis):
    return lax.all_to_all(x, axis, 0, 0, tiled=True)


def local(f, vel_index, signs, cell_type, coupling):
    members = lax.axis_size("vert")
    table, cross = velocity_tables(vel_index, signs, coupling)
    fluid = jnp.where(cell_type == 1, 0.0, 1.0).astype(F32)
    walls = wall_rows(cell_type, lax.axis_index("vert"))
    own = lax.axis_index("gx") * 4 + lax.axis_index(GY)
    place = jnp.stack([own, lax.axis_index("core")]).astype(jnp.int32)
    win_one, north, south = stage_first(f, table, members)
    got_one = swap_all(win_one, "vert")
    near = halos(f, north, south)
    near, got_one = lax.optimization_barrier((near, got_one))
    g, win_two, north, south = stage_second(f, table, *near, fluid, cross, members)
    got_two = swap_all(win_two, "vert")
    near = halos(g, north, south)
    whole, coef = stage_middle(got_one, got_two, walls)
    this_core = swap_all(whole, ("gx", "zh"))
    that_core = lax.ppermute(this_core, "core", [(0, 1), (1, 0)])
    sent = stage_solve(place, this_core, that_core, coef, members)
    got = swap_all(sent, "vert")
    return stage_last(table, got, g, *near, fluid)


def solution(mesh):
    in_specs = (
        P("vert", "gx", GY, None),
        P(None, "vert"),
        P(None, "vert"),
        P("gx", GY, None),
        P(),
    )
    out_specs = P("vert", "gx", GY, None)
    fine_mesh = Mesh(mesh.devices.reshape(4, 2, 2, -1), ("gx",) + GY + ("vert",))
    return jax.shard_map(
        local, mesh=fine_mesh, in_specs=in_specs, out_specs=out_specs, check_vma=False
    )
```

```python
import jax
import jax.numpy as jnp
import numpy as np
from jax import lax
from jax.experimental import pallas as pl
from jax.experimental.pallas import tpu as pltpu
from jax.sharding import Mesh
from jax.sharding import PartitionSpec as P


V = 1024
INTERPRET = False
LAST, SECOND, MOMENTS = 2, 8, 8

absorb = 0.5
damping = 0.8
fine_diag = 6.5
prandtl = 2.0 / 3.0

SX, SY, NZ = 4, 8, 128
COLS = SX * SY
ROWS = 8
LANES = ROWS * COLS
BLOCKS = 16
WIN = 24
WIN2 = 16
F32 = jnp.float32


def roll(x, shift, axis):
    return pltpu.roll(x, shift % x.shape[axis], axis)


def iota(shape, dim):
    return lax.broadcasted_iota(jnp.int32, shape, dim)


def velocity_tables(vel_index, signs, coupling):
    speeds = (vel_index.astype(F32) + 0.5) * 0.25
    positive = signs.astype(F32)
    veloc = speeds * (positive * 2.0 - 1.0)
    square = jnp.sum(veloc * veloc, axis=0)
    weight = 64.0 * jnp.exp(-square) / V
    vel_x, vel_y, vel_z = (veloc[0], veloc[1], veloc[2])
    unit_row = jnp.ones_like(vel_x)
    heat_term = square - 2.5
    basis = (
        jnp.stack(
            [
                unit_row,
                vel_x,
                vel_y,
                vel_z,
                square - 1.5,
                vel_x * vel_y,
                vel_x * vel_z,
                vel_y * vel_z,
                vel_x * vel_x - vel_y * vel_y,
                vel_y * vel_y - vel_z * vel_z,
                heat_term * vel_x,
                heat_term * vel_y,
                heat_term * vel_z,
            ]
        )
        * weight[None]
    )
    shakhov = 0.8 * (1.0 - prandtl)
    equil = jnp.stack(
        [
            unit_row,
            2.0 * vel_x,
            2.0 * vel_y,
            2.0 * vel_z,
            2.0 / 3.0 * (square - 1.5),
            shakhov * heat_term * vel_x,
            shakhov * heat_term * vel_y,
            shakhov * heat_term * vel_z,
        ]
    )
    mixed = jnp.sum(coupling[:, :, None] * basis[None, 5:13], axis=1)
    source_basis = jnp.concatenate([absorb * basis[0:5] + mixed, basis[10:13]], axis=0)
    centre = 0.5 - 0.3 * jnp.sum(speeds, axis=0)
    table = jnp.concatenate(
        [
            source_basis,
            equil,
            centre[None],
            0.4 * speeds * positive,
            0.4 * speeds * (1.0 - positive),
            jnp.zeros_like(centre)[None],
        ],
        axis=0,
    )
    cross = jnp.sum(source_basis[:, None] * equil[None], axis=2)
    cross_row = jnp.pad(cross, ((0, 0), (0, COLS - ROWS))).reshape(1, LANES)
    return table, cross_row


def moments(src, table, m_scr, ext):
    zero = jnp.zeros((SY, NZ), F32)

    def step(v, accs):
        tiles = [src[v, x] for x in range(SX)]
        out = []
        for r in range(ROWS):
            w = table[r, v]
            out += [accs[r * SX + x] + w * tiles[x] for x in range(SX)]
        return tuple(out)

    accs = lax.fori_loop(0, src.shape[0], step, (zero,) * (ROWS * SX), unroll=MOMENTS)
    for i, acc in enumerate(accs):
        m_scr[i * SY : (i + 1) * SY, :] = acc
    for h in range(2):
        turned = m_scr[h * 128 : (h + 1) * 128, :].T
        lanes = slice(h * 128, (h + 1) * 128)
        ext[16:144, lanes] = turned
        ext[0:16, lanes] = turned[112:128]
        ext[144:168, lanes] = turned[0:24]


def first_kernel(table, f, win, north, south, m_scr, ext):
    moments(f, table, m_scr, ext)
    for j in range(win.shape[0]):
        win[j] = ext[4 * j + 6 : 4 * j + 6 + WIN, :]
    pack_rows(f, north, south)


def pack_rows(src, north, south):
    pair = iota((SY, NZ), 0) // 2

    def step(v, carry):
        top = roll(src[v, 0], 0, 0)
        low = roll(src[v, 0], -6, 0)
        for x in range(1, SX):
            tile = src[v, x]
            top = jnp.where(pair == x, roll(tile, 2 * x, 0), top)
            low = jnp.where(pair == x, roll(tile, 2 * x - 6, 0), low)
        north[v] = top
        south[v] = low
        return carry

    lax.fori_loop(0, src.shape[0], step, 0, unroll=4)


def row_halo(north, south, x, sub):
    return jnp.where(sub < 4, roll(north, -2 * x, 0), roll(south, 6 - 2 * x, 0))


def transport(table, v, tiles, edges, sub):
    centre = table[16, v]
    up = [table[17 + d, v] for d in range(3)]
    down = [table[20 + d, v] for d in range(3)]
    out = []
    for x in range(SX):
        f = tiles[x + 2]
        e = edges[x]
        acc = centre * f
        acc += up[0] * (tiles[x + 1] - 0.25 * tiles[x])
        acc += down[0] * (tiles[x + 3] - 0.25 * tiles[x + 4])
        back_one = roll(jnp.where(sub >= 7, e, f), 1, 0)
        back_two = roll(jnp.where(sub >= 6, e, f), 2, 0)
        front_one = roll(jnp.where(sub < 1, e, f), -1, 0)
        front_two = roll(jnp.where(sub < 2, e, f), -2, 0)
        acc += up[1] * (back_one - 0.25 * back_two)
        acc += down[1] * (front_one - 0.25 * front_two)
        acc += up[2] * (roll(f, 1, 1) - 0.25 * roll(f, 2, 1))
        acc += down[2] * (roll(f, -1, 1) - 0.25 * roll(f, -2, 1))
        out.append(acc)
    return out


def second_kernel(table, f, low, high, north, south, fluid, cross, g, win, g_north, g_south, m_scr, ext):
    sub = iota((SY, NZ), 0)

    def step(v, carry):
        tiles = [low[v, 0], low[v, 1]] + [f[v, x] for x in range(SX)] + [high[v, 0], high[v, 1]]
        above, below = north[v], south[v]
        edges = [row_halo(above, below, x, sub) for x in range(SX)]
        moved = transport(table, v, tiles, edges, sub)
        for x in range(SX):
            g[v, x] = fluid[x] * moved[x]
        return carry

    lax.fori_loop(0, f.shape[0], step, 0, unroll=SECOND)
    moments(g, table, m_scr, ext)
    for j in range(win.shape[0]):
        win[j] = ext[4 * j + 10 : 4 * j + 10 + WIN2, :]
        win[j, 0:1, :] = cross[...]
    pack_rows(g, g_north, g_south)


def neighbours(ref, k, around, step, low, rows):
    lane = iota((rows, 128), 1)
    x_at, y_at = (lane // SY) % SX, lane % SY

    def load(q, shift=0):
        return ref[q, 8 + low + shift : 8 + low + shift + rows, :]

    c = load(k)
    dx, dy = SY * step, step
    if len(around) == 4:
        up, down = roll(load(around[2]), SY - dy, 1), roll(load(around[3]), dy - SY, 1)
    else:
        up, down = roll(c, SY - COLS - dy, 1), roll(c, COLS - SY + dy, 1)
    total = jnp.where(x_at < SX - step, roll(c, -dx, 1), roll(load(around[0]), COLS - dx, 1))
    total += jnp.where(x_at >= step, roll(c, dx, 1), roll(load(around[1]), dx - COLS, 1))
    total += jnp.where(y_at < SY - step, roll(c, -dy, 1), up)
    total += jnp.where(y_at >= step, roll(c, dy, 1), down)
    return total + load(k, step) + load(k, -step)


def around_block(i):
    gx, gy = i // 4, i % 4
    return (
        ((gx + 1) % 4) * 4 + gy,
        ((gx + 3) % 4) * 4 + gy,
        gx * 4 + (gy + 1) % 4,
        gx * 4 + (gy + 3) % 4,
    )


def around_packed(gx):
    return (BLOCKS + (gx + 1) % 4, BLOCKS + (gx + 3) % 4)


EVERY = [(i, around_block(i)) for i in range(BLOCKS)]
EVERY += [(BLOCKS + gx, around_packed(gx)) for gx in range(4)]


def restrict(src, coarse, k, around, rows):
    lane = iota((rows, 128), 1)
    c = src[k, 8 : 8 + rows, :]
    r = (1.0 - damping) * c + (damping / fine_diag) * neighbours(src, k, around, 1, 0, rows)
    r = r + jnp.where((lane // SY) % 2 == 0, roll(r, -SY, 1), roll(r, SY, 1))
    r = r + jnp.where(lane % 2 == 0, roll(r, -1, 1), roll(r, 1, 1))
    r = r + jnp.where(iota((rows, 128), 0) % 2 == 0, roll(r, -1, 0), roll(r, 1, 0))
    coarse[k, 8 : 8 + rows, :] = 0.125 * r


def correct(src, coarse, fine, k, around, rows):
    span = slice(8, 8 + rows)
    two = 0.48 * coarse[k, span, :] + 0.04 * neighbours(coarse, k, around, 2, 0, rows)
    fine[k, span, :] = (damping / fine_diag) * src[k, span, :] + two


def smooth(src, fine, k, around, low, rows):
    span = slice(8 + low, 8 + low + rows)
    return (1.0 - damping) * fine[k, span, :] + (damping / fine_diag) * (
        src[k, span, :] + neighbours(fine, k, around, 1, low, rows)
    )


def solve_kernel(place, near, far, coef, out, src, coarse, fine, tail, gain, extra, field, msg):
    tile_sub = iota((8, 128), 0)
    tile_lane = iota((8, 128), 1)
    lane = iota((WIN2, 128), 1)
    group = lane // COLS

    def pack(ref, rows):
        where = iota((rows, 128), 1) // COLS
        for gx in range(4):
            packed = ref[4 * gx, 0:rows, :]
            for gy in range(1, 4):
                moved = roll(ref[4 * gx + gy, 0:rows, :], COLS * gy, 1)
                packed = jnp.where(where == gy, moved, packed)
            src[BLOCKS + gx, 8 : 8 + rows, :] = packed

    for i in range(BLOCKS):
        rows = jnp.where(i % 2 == place[1], near[i // 2], far[i // 2])
        src[i, 8 : 8 + WIN, :] = rows[0:WIN, 0:128]
        tail[i] = rows[0:WIN, 128:256]
        for h in range(2):
            extra[i, h] = rows[WIN : WIN + WIN2, h * 128 : (h + 1) * 128]
        for half, at in enumerate((WIN, WIN + WIN2 - 1)):
            left = jnp.broadcast_to(rows[at : at + 1, 0:128], (8, 128))
            right = jnp.broadcast_to(rows[at : at + 1, 128:256], (8, 128))
            t = jnp.where(tile_sub < 4, left, right)
            t = jnp.where(tile_lane // COLS == tile_sub % 4, t, 0.0)
            t = t + roll(t, 32, 1)
            gain[i, 8 * half : 8 * half + 8, :] = t + roll(t, 64, 1)
    pack(tail, WIN)
    for k, around in EVERY:
        restrict(src, coarse, k, around, WIN)
    for k, around in EVERY:
        correct(src, coarse, fine, k, around, WIN)
    for k, around in EVERY[:BLOCKS]:
        field[k, 0] = smooth(src, fine, k, around, 4, WIN2)
    for gx in range(4):
        packed = smooth(src, fine, BLOCKS + gx, around_packed(gx), 4, WIN2)
        for gy in range(4):
            moved = roll(packed, -COLS * gy, 1) if gy else packed
            i = 4 * gx + gy
            field[i, 1] = jnp.where(group == 0, moved, tail[i, 4 : 4 + WIN2, :])
    for i in range(BLOCKS):
        parts = (field[i, 0], field[i, 1])
        sums = [0.0, 0.0]
        for b in range(4):
            turned = [roll(p, -COLS * b, 1) if b else p for p in parts]
            same = turned
            if b:
                inside = lane < 128 - COLS * b
                same = [
                    jnp.where(inside, turned[0], turned[1]),
                    jnp.where(inside, turned[1], turned[0]),
                ]
            for h in range(2):
                lanes = slice(h * 128, (h + 1) * 128)
                sums[h] = (
                    sums[h]
                    + coef[b : b + 1, lanes] * same[h]
                    + coef[4 + b : 5 + b, lanes] * same[1 - h]
                )
        src[i, 8 : 8 + WIN2, :] = gain[i] * sums[0] + extra[i, 0]
        tail[i, 0:WIN2, :] = gain[i] * sums[1] + extra[i, 1]
    pack(tail, WIN2)
    for k, around in EVERY:
        restrict(src, coarse, k, around, WIN2)
    own = place[0]
    own_x = own // 4
    next_x, last_x, next_y, last_y = around_block(own)
    for i in (own, next_x, last_x, next_y, last_y):
        correct(src, coarse, fine, i, around_block(i), WIN2)
    for gx in (own_x, (own_x + 1) % 4, (own_x + 3) % 4):
        correct(src, coarse, fine, BLOCKS + gx, around_packed(gx), WIN2)
    packed = smooth(src, fine, BLOCKS + own_x, around_packed(own_x), 0, WIN2)
    moved = packed
    for gy in range(1, 4):
        moved = jnp.where(own % 4 == gy, roll(packed, -COLS * gy, 1), moved)
    second = (
        smooth(src, fine, own, around_block(own), 0, WIN2),
        jnp.where(group == 0, moved, tail[own, 0:WIN2, :]),
    )
    x_at, y_at = (lane // SY) % SX, lane % SY

    def first(i, h):
        return gain[i] * field[i, h]

    for h in range(2):
        side_x = jnp.where(
            x_at < 2, roll(first(last_x, h), -16, 1), roll(first(next_x, h), 16, 1)
        )
        side_y = jnp.where(y_at < 4, first(next_y, h), first(last_y, h))
        pieces = ((first(own, h), side_x), (side_y, gain[own] * second[h]))
        for k in range(2):
            for m in range(2):
                at = (2 * m + h) * 128
                spot = 4 * k + 2 * m + h
                coarse[spot, 8 : 8 + WIN2, :] = pieces[k][m]
                msg[4 * k : 4 * k + 4, at : at + 128] = coarse[spot, 14:18, :]
    for j in range(out.shape[0]):
        out[j] = msg[...]


def last_kernel(table, recv, g, low, high, north, south, fluid, out, turn, fields):
    for j in range(recv.shape[0]):
        turn[4 * j : 4 * j + 4, 0:512] = recv[j, 0:4, :]
        turn[4 * j : 4 * j + 4, 512:1024] = recv[j, 4:8, :]
    for k in range(8):
        block = turn[:, k * 128 : (k + 1) * 128].T
        for r in range(4):
            for x in range(SX):
                at = (r * SX + x) * SY
                fields[k // 2, (k % 2) * 4 + r, x] = block[at : at + SY]
    sub = iota((SY, NZ), 0)

    def step(v, carry):
        psi = [table[ROWS + r, v] for r in range(ROWS)]

        def lift(part, x):
            total = psi[0] * fields[part, 0, x]
            for r in range(1, ROWS):
                total += psi[r] * fields[part, r, x]
            return total

        above, below = north[v], south[v]
        tiles = [lift(1, x) + low[v, x] for x in range(2)]
        tiles += [lift(0, x) + g[v, x] for x in range(SX)]
        tiles += [lift(1, 2 + x) + high[v, x] for x in range(2)]
        edges = [lift(2, x) + row_halo(above, below, x, sub) for x in range(SX)]
        moved = transport(table, v, tiles, edges, sub)
        for x in range(SX):
            out[v, x] = fluid[x] * moved[x] + lift(3, x)
        return carry

    lax.fori_loop(0, out.shape[0], step, 0, unroll=LAST)


GY = ("zh", "core")
VMEM = pltpu.MemorySpace.VMEM
SMEM = pltpu.MemorySpace.SMEM


def call(kernel, spaces, outs, scratch):
    specs = [pl.BlockSpec(memory_space=s) for s in spaces]
    shapes = [jax.ShapeDtypeStruct(s, F32) for s in outs]
    return pl.pallas_call(
        kernel,
        in_specs=specs,
        out_specs=[pl.BlockSpec(memory_space=VMEM) for _ in outs],
        out_shape=shapes,
        scratch_shapes=[pltpu.VMEM(s, F32) for s in scratch],
        interpret=INTERPRET,
    )


def stage_first(f, table, members):
    vels = f.shape[0]
    return call(
        first_kernel,
        (SMEM, VMEM),
        ((members, WIN, LANES), (vels, SY, NZ), (vels, SY, NZ)),
        ((LANES, NZ), (168, LANES)),
    )(table, f)


def stage_second(f, table, low, high, north, south, fluid, cross, members):
    vels = f.shape[0]
    return call(
        second_kernel,
        (SMEM,) + (VMEM,) * 7,
        (f.shape, (members, WIN2, LANES), (vels, SY, NZ), (vels, SY, NZ)),
        ((LANES, NZ), (168, LANES)),
    )(table, f, low, high, north, south, fluid, cross)


def wall_rows(cell_type, member):
    gain = jnp.where(cell_type == 1, 1.0, 0.5).astype(F32).reshape(COLS, NZ).T
    wrapped = jnp.concatenate([gain[NZ - 8 :], gain, gain[:16]], axis=0)
    return lax.dynamic_slice_in_dim(wrapped, 4 * member + 2, WIN2, axis=0).reshape(2, LANES)


def stage_middle(got_one, got_two, walls):
    one = jnp.sum(got_one, axis=0)
    two = jnp.sum(got_two, axis=0)
    whole = jnp.concatenate([one, walls[0:1], two[1 : WIN2 - 1], walls[1:2]], axis=0)
    cross = two[0].reshape(ROWS, COLS)[:, :ROWS]
    pick = np.zeros((ROWS, ROWS, ROWS), np.float32)
    for k in range(ROWS):
        for r in range(ROWS):
            pick[k, r, (r + k) % ROWS] = 1.0
    coef = jnp.sum(jnp.asarray(pick) * cross[None], axis=2)
    coef = jnp.broadcast_to(coef[:, :, None], (ROWS, ROWS, COLS)).reshape(ROWS, LANES)
    return jnp.broadcast_to(whole[None], (BLOCKS // 2,) + whole.shape), coef


def stage_solve(place, near, far, coef, members):
    padded = (BLOCKS + 4, WIN + 16, 128)
    half = (BLOCKS, WIN2, 128)
    pair = (BLOCKS, 2, WIN2, 128)
    return call(
        solve_kernel,
        (SMEM, VMEM, VMEM, VMEM),
        ((members, 8, 512),),
        (padded,) * 3 + ((BLOCKS, WIN, 128), half, pair, pair, (8, 512)),
    )(place, near, far, coef)[0]


def stage_last(table, got, g, low, high, north, south, fluid):
    return call(
        last_kernel,
        (SMEM,) + (VMEM,) * 7,
        (g.shape,),
        ((NZ, 1024), (4, ROWS, SX, SY, NZ)),
    )(table, got, g, low, high, north, south, fluid)[0]


def halos(f, north, south):
    def ring(axis, step):
        count = lax.axis_size(axis)
        return [(i, (i + step) % count) for i in range(count)]

    low = lax.ppermute(f[:, SX - 2 :], "gx", ring("gx", 1))
    high = lax.ppermute(f[:, :2], "gx", ring("gx", -1))
    above = lax.ppermute(north, GY, ring(GY, -1))
    below = lax.ppermute(south, GY, ring(GY, 1))
    return low, high, above, below


def swap_all(x, axis):
    return lax.all_to_all(x, axis, 0, 0, tiled=True)


def local(f, vel_index, signs, cell_type, coupling):
    members = lax.axis_size("vert")
    table, cross = velocity_tables(vel_index, signs, coupling)
    fluid = jnp.where(cell_type == 1, 0.0, 1.0).astype(F32)
    walls = wall_rows(cell_type, lax.axis_index("vert"))
    own = lax.axis_index("gx") * 4 + lax.axis_index(GY)
    place = jnp.stack([own, lax.axis_index("core")]).astype(jnp.int32)
    win_one, north, south = stage_first(f, table, members)
    got_one = swap_all(win_one, "vert")
    near = halos(f, north, south)
    near, got_one = lax.optimization_barrier((near, got_one))
    g, win_two, north, south = stage_second(f, table, *near, fluid, cross, members)
    got_two = swap_all(win_two, "vert")
    near = halos(g, north, south)
    whole, coef = stage_middle(got_one, got_two, walls)
    this_core = swap_all(whole, ("gx", "zh"))
    that_core = lax.ppermute(this_core, "core", [(0, 1), (1, 0)])
    sent = stage_solve(place, this_core, that_core, coef, members)
    got = swap_all(sent, "vert")
    return stage_last(table, got, g, *near, fluid)


def solution(mesh):
    in_specs = (
        P("vert", "gx", GY, None),
        P(None, "vert"),
        P(None, "vert"),
        P("gx", GY, None),
        P(),
    )
    out_specs = P("vert", "gx", GY, None)
    fine_mesh = Mesh(mesh.devices.reshape(4, 2, 2, -1), ("gx",) + GY + ("vert",))
    return jax.shard_map(
        local, mesh=fine_mesh, in_specs=in_specs, out_specs=out_specs, check_vma=False
    )
```

```python
import jax
import jax.numpy as jnp
import numpy as np
from jax import lax
from jax.experimental import pallas as pl
from jax.experimental.pallas import tpu as pltpu
from jax.sharding import Mesh
from jax.sharding import PartitionSpec as P


V = 1024
INTERPRET = False
LAST, SECOND, MOMENTS = 2, 8, 8

absorb = 0.5
damping = 0.8
fine_diag = 6.5
prandtl = 2.0 / 3.0

SX, SY, NZ = 4, 8, 128
COLS = SX * SY
ROWS = 8
LANES = ROWS * COLS
BLOCKS = 16
WIN = 24
WIN2 = 16
F32 = jnp.float32


def roll(x, shift, axis):
    return pltpu.roll(x, shift % x.shape[axis], axis)


def iota(shape, dim):
    return lax.broadcasted_iota(jnp.int32, shape, dim)


def velocity_tables(vel_index, signs, coupling):
    speeds = (vel_index.astype(F32) + 0.5) * 0.25
    positive = signs.astype(F32)
    veloc = speeds * (positive * 2.0 - 1.0)
    square = jnp.sum(veloc * veloc, axis=0)
    weight = 64.0 * jnp.exp(-square) / V
    vel_x, vel_y, vel_z = (veloc[0], veloc[1], veloc[2])
    unit_row = jnp.ones_like(vel_x)
    heat_term = square - 2.5
    basis = (
        jnp.stack(
            [
                unit_row,
                vel_x,
                vel_y,
                vel_z,
                square - 1.5,
                vel_x * vel_y,
                vel_x * vel_z,
                vel_y * vel_z,
                vel_x * vel_x - vel_y * vel_y,
                vel_y * vel_y - vel_z * vel_z,
                heat_term * vel_x,
                heat_term * vel_y,
                heat_term * vel_z,
            ]
        )
        * weight[None]
    )
    shakhov = 0.8 * (1.0 - prandtl)
    equil = jnp.stack(
        [
            unit_row,
            2.0 * vel_x,
            2.0 * vel_y,
            2.0 * vel_z,
            2.0 / 3.0 * (square - 1.5),
            shakhov * heat_term * vel_x,
            shakhov * heat_term * vel_y,
            shakhov * heat_term * vel_z,
        ]
    )
    mixed = jnp.sum(coupling[:, :, None] * basis[None, 5:13], axis=1)
    source_basis = jnp.concatenate([absorb * basis[0:5] + mixed, basis[10:13]], axis=0)
    centre = 0.5 - 0.3 * jnp.sum(speeds, axis=0)
    table = jnp.concatenate(
        [
            source_basis,
            equil,
            centre[None],
            0.4 * speeds * positive,
            0.4 * speeds * (1.0 - positive),
            jnp.zeros_like(centre)[None],
        ],
        axis=0,
    )
    cross = jnp.sum(source_basis[:, None] * equil[None], axis=2)
    cross_row = jnp.pad(cross, ((0, 0), (0, COLS - ROWS))).reshape(1, LANES)
    return table, cross_row


def moments(src, table, m_scr, ext):
    zero = jnp.zeros((SY, NZ), F32)

    def step(v, accs):
        tiles = [src[v, x] for x in range(SX)]
        out = []
        for r in range(ROWS):
            w = table[r, v]
            out += [accs[r * SX + x] + w * tiles[x] for x in range(SX)]
        return tuple(out)

    accs = lax.fori_loop(0, src.shape[0], step, (zero,) * (ROWS * SX), unroll=MOMENTS)
    for i, acc in enumerate(accs):
        m_scr[i * SY : (i + 1) * SY, :] = acc
    for h in range(2):
        turned = m_scr[h * 128 : (h + 1) * 128, :].T
        lanes = slice(h * 128, (h + 1) * 128)
        ext[16:144, lanes] = turned
        ext[0:16, lanes] = turned[112:128]
        ext[144:168, lanes] = turned[0:24]


def first_kernel(table, f, win, north, south, m_scr, ext):
    moments(f, table, m_scr, ext)
    for j in range(win.shape[0]):
        win[j] = ext[4 * j + 6 : 4 * j + 6 + WIN, :]
    pack_rows(f, north, south)


def pack_rows(src, north, south):
    pair = iota((SY, NZ), 0) // 2

    def step(v, carry):
        top = roll(src[v, 0], 0, 0)
        low = roll(src[v, 0], -6, 0)
        for x in range(1, SX):
            tile = src[v, x]
            top = jnp.where(pair == x, roll(tile, 2 * x, 0), top)
            low = jnp.where(pair == x, roll(tile, 2 * x - 6, 0), low)
        north[v] = top
        south[v] = low
        return carry

    lax.fori_loop(0, src.shape[0], step, 0, unroll=4)


def row_halo(north, south, x, sub):
    return jnp.where(sub < 4, roll(north, -2 * x, 0), roll(south, 6 - 2 * x, 0))


def transport(table, v, tiles, edges, sub):
    centre = table[16, v]
    up = [table[17 + d, v] for d in range(3)]
    down = [table[20 + d, v] for d in range(3)]
    out = []
    for x in range(SX):
        f = tiles[x + 2]
        e = edges[x]
        acc = centre * f
        acc += up[0] * (tiles[x + 1] - 0.25 * tiles[x])
        acc += down[0] * (tiles[x + 3] - 0.25 * tiles[x + 4])
        back_one = roll(jnp.where(sub >= 7, e, f), 1, 0)
        back_two = roll(jnp.where(sub >= 6, e, f), 2, 0)
        front_one = roll(jnp.where(sub < 1, e, f), -1, 0)
        front_two = roll(jnp.where(sub < 2, e, f), -2, 0)
        acc += up[1] * (back_one - 0.25 * back_two)
        acc += down[1] * (front_one - 0.25 * front_two)
        acc += up[2] * (roll(f, 1, 1) - 0.25 * roll(f, 2, 1))
        acc += down[2] * (roll(f, -1, 1) - 0.25 * roll(f, -2, 1))
        out.append(acc)
    return out


def second_kernel(table, f, low, high, north, south, fluid, cross, g, win, g_north, g_south, m_scr, ext):
    sub = iota((SY, NZ), 0)

    def step(v, carry):
        tiles = [low[v, 0], low[v, 1]] + [f[v, x] for x in range(SX)] + [high[v, 0], high[v, 1]]
        above, below = north[v], south[v]
        edges = [row_halo(above, below, x, sub) for x in range(SX)]
        moved = transport(table, v, tiles, edges, sub)
        for x in range(SX):
            g[v, x] = fluid[x] * moved[x]
        return carry

    lax.fori_loop(0, f.shape[0], step, 0, unroll=SECOND)
    moments(g, table, m_scr, ext)
    for j in range(win.shape[0]):
        win[j] = ext[4 * j + 10 : 4 * j + 10 + WIN2, :]
        win[j, 0:1, :] = cross[...]
    pack_rows(g, g_north, g_south)


def neighbours(ref, k, around, step, low, rows):
    lane = iota((rows, 128), 1)
    x_at, y_at = (lane // SY) % SX, lane % SY

    def load(q, shift=0):
        return ref[q, 8 + low + shift : 8 + low + shift + rows, :]

    c = load(k)
    dx, dy = SY * step, step
    if len(around) == 4:
        up, down = roll(load(around[2]), SY - dy, 1), roll(load(around[3]), dy - SY, 1)
    else:
        up, down = roll(c, SY - COLS - dy, 1), roll(c, COLS - SY + dy, 1)
    total = jnp.where(x_at < SX - step, roll(c, -dx, 1), roll(load(around[0]), COLS - dx, 1))
    total += jnp.where(x_at >= step, roll(c, dx, 1), roll(load(around[1]), dx - COLS, 1))
    total += jnp.where(y_at < SY - step, roll(c, -dy, 1), up)
    total += jnp.where(y_at >= step, roll(c, dy, 1), down)
    return total + load(k, step) + load(k, -step)


def around_block(i):
    gx, gy = i // 4, i % 4
    return (
        ((gx + 1) % 4) * 4 + gy,
        ((gx + 3) % 4) * 4 + gy,
        gx * 4 + (gy + 1) % 4,
        gx * 4 + (gy + 3) % 4,
    )


def around_packed(gx):
    return (BLOCKS + (gx + 1) % 4, BLOCKS + (gx + 3) % 4)


EVERY = [(i, around_block(i)) for i in range(BLOCKS)]
EVERY += [(BLOCKS + gx, around_packed(gx)) for gx in range(4)]


def restrict(src, coarse, spare, rows):
    span = slice(8, 8 + rows)
    lane = iota((rows, 128), 1)
    for k, around in EVERY:
        spare[k, span, :] = (1.0 - damping) * src[k, span, :] + (
            damping / fine_diag
        ) * neighbours(src, k, around, 1, 0, rows)
    for k, around in EVERY:
        r = spare[k, span, :]
        pair = jnp.where((lane // SY) % 2 == 0, roll(r, -SY, 1), roll(r, SY, 1))
        coarse[k, span, :] = r + pair
    for k, around in EVERY:
        r = coarse[k, span, :]
        spare[k, span, :] = r + jnp.where(lane % 2 == 0, roll(r, -1, 1), roll(r, 1, 1))
    for k, around in EVERY:
        above, below = spare[k, 9 : 9 + rows, :], spare[k, 7 : 7 + rows, :]
        pair = jnp.where(iota((rows, 128), 0) % 2 == 0, above, below)
        coarse[k, span, :] = 0.125 * (spare[k, span, :] + pair)


def correct(src, coarse, fine, k, around, rows):
    span = slice(8, 8 + rows)
    two = 0.48 * coarse[k, span, :] + 0.04 * neighbours(coarse, k, around, 2, 0, rows)
    fine[k, span, :] = (damping / fine_diag) * src[k, span, :] + two


def smooth(src, fine, k, around, low, rows):
    span = slice(8 + low, 8 + low + rows)
    return (1.0 - damping) * fine[k, span, :] + (damping / fine_diag) * (
        src[k, span, :] + neighbours(fine, k, around, 1, low, rows)
    )


def solve_kernel(place, near, far, coef, out, src, coarse, fine, tail, gain, extra, field, msg):
    tile_sub = iota((8, 128), 0)
    tile_lane = iota((8, 128), 1)
    lane = iota((WIN2, 128), 1)
    group = lane // COLS

    def pack(ref, rows):
        where = iota((rows, 128), 1) // COLS
        for gx in range(4):
            packed = ref[4 * gx, 0:rows, :]
            for gy in range(1, 4):
                moved = roll(ref[4 * gx + gy, 0:rows, :], COLS * gy, 1)
                packed = jnp.where(where == gy, moved, packed)
            src[BLOCKS + gx, 8 : 8 + rows, :] = packed

    for i in range(BLOCKS):
        rows = jnp.where(i % 2 == place[1], near[i // 2], far[i // 2])
        src[i, 8 : 8 + WIN, :] = rows[0:WIN, 0:128]
        tail[i] = rows[0:WIN, 128:256]
        for h in range(2):
            extra[i, h] = rows[WIN : WIN + WIN2, h * 128 : (h + 1) * 128]
        for half, at in enumerate((WIN, WIN + WIN2 - 1)):
            left = jnp.broadcast_to(rows[at : at + 1, 0:128], (8, 128))
            right = jnp.broadcast_to(rows[at : at + 1, 128:256], (8, 128))
            t = jnp.where(tile_sub < 4, left, right)
            t = jnp.where(tile_lane // COLS == tile_sub % 4, t, 0.0)
            t = t + roll(t, 32, 1)
            gain[i, 8 * half : 8 * half + 8, :] = t + roll(t, 64, 1)
    pack(tail, WIN)
    restrict(src, coarse, fine, WIN)
    for k, around in EVERY:
        correct(src, coarse, fine, k, around, WIN)
    for k, around in EVERY[:BLOCKS]:
        field[k, 0] = smooth(src, fine, k, around, 4, WIN2)
    for gx in range(4):
        packed = smooth(src, fine, BLOCKS + gx, around_packed(gx), 4, WIN2)
        for gy in range(4):
            moved = roll(packed, -COLS * gy, 1) if gy else packed
            i = 4 * gx + gy
            field[i, 1] = jnp.where(group == 0, moved, tail[i, 4 : 4 + WIN2, :])
    for i in range(BLOCKS):
        parts = (field[i, 0], field[i, 1])
        sums = [0.0, 0.0]
        for b in range(4):
            turned = [roll(p, -COLS * b, 1) if b else p for p in parts]
            same = turned
            if b:
                inside = lane < 128 - COLS * b
                same = [
                    jnp.where(inside, turned[0], turned[1]),
                    jnp.where(inside, turned[1], turned[0]),
                ]
            for h in range(2):
                lanes = slice(h * 128, (h + 1) * 128)
                sums[h] = (
                    sums[h]
                    + coef[b : b + 1, lanes] * same[h]
                    + coef[4 + b : 5 + b, lanes] * same[1 - h]
                )
        src[i, 8 : 8 + WIN2, :] = gain[i] * sums[0] + extra[i, 0]
        tail[i, 0:WIN2, :] = gain[i] * sums[1] + extra[i, 1]
    pack(tail, WIN2)
    restrict(src, coarse, fine, WIN2)
    own = place[0]
    own_x = own // 4
    next_x, last_x, next_y, last_y = around_block(own)
    for i in (own, next_x, last_x, next_y, last_y):
        correct(src, coarse, fine, i, around_block(i), WIN2)
    for gx in (own_x, (own_x + 1) % 4, (own_x + 3) % 4):
        correct(src, coarse, fine, BLOCKS + gx, around_packed(gx), WIN2)
    packed = smooth(src, fine, BLOCKS + own_x, around_packed(own_x), 0, WIN2)
    moved = packed
    for gy in range(1, 4):
        moved = jnp.where(own % 4 == gy, roll(packed, -COLS * gy, 1), moved)
    second = (
        smooth(src, fine, own, around_block(own), 0, WIN2),
        jnp.where(group == 0, moved, tail[own, 0:WIN2, :]),
    )
    x_at, y_at = (lane // SY) % SX, lane % SY

    def first(i, h):
        return gain[i] * field[i, h]

    for h in range(2):
        side_x = jnp.where(
            x_at < 2, roll(first(last_x, h), -16, 1), roll(first(next_x, h), 16, 1)
        )
        side_y = jnp.where(y_at < 4, first(next_y, h), first(last_y, h))
        pieces = ((first(own, h), side_x), (side_y, gain[own] * second[h]))
        for k in range(2):
            for m in range(2):
                at = (2 * m + h) * 128
                spot = 4 * k + 2 * m + h
                coarse[spot, 8 : 8 + WIN2, :] = pieces[k][m]
                msg[4 * k : 4 * k + 4, at : at + 128] = coarse[spot, 14:18, :]
    for j in range(out.shape[0]):
        out[j] = msg[...]


def last_kernel(table, recv, g, low, high, north, south, fluid, out, turn, fields):
    for j in range(recv.shape[0]):
        turn[4 * j : 4 * j + 4, 0:512] = recv[j, 0:4, :]
        turn[4 * j : 4 * j + 4, 512:1024] = recv[j, 4:8, :]
    for k in range(8):
        block = turn[:, k * 128 : (k + 1) * 128].T
        for r in range(4):
            for x in range(SX):
                at = (r * SX + x) * SY
                fields[k // 2, (k % 2) * 4 + r, x] = block[at : at + SY]
    sub = iota((SY, NZ), 0)

    def step(v, carry):
        psi = [table[ROWS + r, v] for r in range(ROWS)]

        def lift(part, x):
            total = psi[0] * fields[part, 0, x]
            for r in range(1, ROWS):
                total += psi[r] * fields[part, r, x]
            return total

        above, below = north[v], south[v]
        tiles = [lift(1, x) + low[v, x] for x in range(2)]
        tiles += [lift(0, x) + g[v, x] for x in range(SX)]
        tiles += [lift(1, 2 + x) + high[v, x] for x in range(2)]
        edges = [lift(2, x) + row_halo(above, below, x, sub) for x in range(SX)]
        moved = transport(table, v, tiles, edges, sub)
        for x in range(SX):
            out[v, x] = fluid[x] * moved[x] + lift(3, x)
        return carry

    lax.fori_loop(0, out.shape[0], step, 0, unroll=LAST)


GY = ("zh", "core")
VMEM = pltpu.MemorySpace.VMEM
SMEM = pltpu.MemorySpace.SMEM


def call(kernel, spaces, outs, scratch):
    specs = [pl.BlockSpec(memory_space=s) for s in spaces]
    shapes = [jax.ShapeDtypeStruct(s, F32) for s in outs]
    return pl.pallas_call(
        kernel,
        in_specs=specs,
        out_specs=[pl.BlockSpec(memory_space=VMEM) for _ in outs],
        out_shape=shapes,
        scratch_shapes=[pltpu.VMEM(s, F32) for s in scratch],
        interpret=INTERPRET,
    )


def stage_first(f, table, members):
    vels = f.shape[0]
    return call(
        first_kernel,
        (SMEM, VMEM),
        ((members, WIN, LANES), (vels, SY, NZ), (vels, SY, NZ)),
        ((LANES, NZ), (168, LANES)),
    )(table, f)


def stage_second(f, table, low, high, north, south, fluid, cross, members):
    vels = f.shape[0]
    return call(
        second_kernel,
        (SMEM,) + (VMEM,) * 7,
        (f.shape, (members, WIN2, LANES), (vels, SY, NZ), (vels, SY, NZ)),
        ((LANES, NZ), (168, LANES)),
    )(table, f, low, high, north, south, fluid, cross)


def wall_rows(cell_type, member):
    gain = jnp.where(cell_type == 1, 1.0, 0.5).astype(F32).reshape(COLS, NZ).T
    wrapped = jnp.concatenate([gain[NZ - 8 :], gain, gain[:16]], axis=0)
    return lax.dynamic_slice_in_dim(wrapped, 4 * member + 2, WIN2, axis=0).reshape(2, LANES)


def stage_middle(got_one, got_two, walls):
    one = jnp.sum(got_one, axis=0)
    two = jnp.sum(got_two, axis=0)
    whole = jnp.concatenate([one, walls[0:1], two[1 : WIN2 - 1], walls[1:2]], axis=0)
    cross = two[0].reshape(ROWS, COLS)[:, :ROWS]
    pick = np.zeros((ROWS, ROWS, ROWS), np.float32)
    for k in range(ROWS):
        for r in range(ROWS):
            pick[k, r, (r + k) % ROWS] = 1.0
    coef = jnp.sum(jnp.asarray(pick) * cross[None], axis=2)
    coef = jnp.broadcast_to(coef[:, :, None], (ROWS, ROWS, COLS)).reshape(ROWS, LANES)
    return jnp.broadcast_to(whole[None], (BLOCKS // 2,) + whole.shape), coef


def stage_solve(place, near, far, coef, members):
    padded = (BLOCKS + 4, WIN + 16, 128)
    half = (BLOCKS, WIN2, 128)
    pair = (BLOCKS, 2, WIN2, 128)
    return call(
        solve_kernel,
        (SMEM, VMEM, VMEM, VMEM),
        ((members, 8, 512),),
        (padded,) * 3 + ((BLOCKS, WIN, 128), half, pair, pair, (8, 512)),
    )(place, near, far, coef)[0]


def stage_last(table, got, g, low, high, north, south, fluid):
    return call(
        last_kernel,
        (SMEM,) + (VMEM,) * 7,
        (g.shape,),
        ((NZ, 1024), (4, ROWS, SX, SY, NZ)),
    )(table, got, g, low, high, north, south, fluid)[0]


def halos(f, north, south):
    def ring(axis, step):
        count = lax.axis_size(axis)
        return [(i, (i + step) % count) for i in range(count)]

    low = lax.ppermute(f[:, SX - 2 :], "gx", ring("gx", 1))
    high = lax.ppermute(f[:, :2], "gx", ring("gx", -1))
    above = lax.ppermute(north, GY, ring(GY, -1))
    below = lax.ppermute(south, GY, ring(GY, 1))
    return low, high, above, below


def swap_all(x, axis):
    return lax.all_to_all(x, axis, 0, 0, tiled=True)


def local(f, vel_index, signs, cell_type, coupling):
    members = lax.axis_size("vert")
    table, cross = velocity_tables(vel_index, signs, coupling)
    fluid = jnp.where(cell_type == 1, 0.0, 1.0).astype(F32)
    walls = wall_rows(cell_type, lax.axis_index("vert"))
    own = lax.axis_index("gx") * 4 + lax.axis_index(GY)
    place = jnp.stack([own, lax.axis_index("core")]).astype(jnp.int32)
    win_one, north, south = stage_first(f, table, members)
    got_one = swap_all(win_one, "vert")
    near = halos(f, north, south)
    near, got_one = lax.optimization_barrier((near, got_one))
    g, win_two, north, south = stage_second(f, table, *near, fluid, cross, members)
    got_two = swap_all(win_two, "vert")
    near = halos(g, north, south)
    whole, coef = stage_middle(got_one, got_two, walls)
    this_core = swap_all(whole, ("gx", "zh"))
    that_core = lax.ppermute(this_core, "core", [(0, 1), (1, 0)])
    sent = stage_solve(place, this_core, that_core, coef, members)
    got = swap_all(sent, "vert")
    return stage_last(table, got, g, *near, fluid)


def solution(mesh):
    in_specs = (
        P("vert", "gx", GY, None),
        P(None, "vert"),
        P(None, "vert"),
        P("gx", GY, None),
        P(),
    )
    out_specs = P("vert", "gx", GY, None)
    fine_mesh = Mesh(mesh.devices.reshape(4, 2, 2, -1), ("gx",) + GY + ("vert",))
    return jax.shard_map(
        local, mesh=fine_mesh, in_specs=in_specs, out_specs=out_specs, check_vma=False
    )
```
